512 devices in a mesh: gx: 32 (over x_hi, z), gy: 16 (over x_lo, y, core).
Axes of the slice: x: 4 (x_hi: 2, x_lo: 2; x = x_hi * 2 + x_lo), y: 4, z: 16, core: 2. Of those that a mesh axis runs over, the one named last changes fastest.
Arguments:
- checkpoint: float32 [27, 8, 128, 2048], P(None, None, 'gx', 'gy'), may hold values from 0.0027 to 0.415, as said below
- rates: float32 [27], replicated, may hold values from 0.8 to 1.7
- wall_mask: int32 [8, 128, 2048], P(None, 'gx', 'gy'), may hold values 0 or 1
- cotangent: float32 [27, 8, 128, 2048], P(None, None, 'gx', 'gy'), may hold values from -6 to 6
Outputs:
- grad_checkpoint: float32 [27, 8, 128, 2048], P(None, None, 'gx', 'gy')
The draws below stay inside these ranges and needn't reach their ends.
Inputs may be any that keep to these rules, and one draw needn't show every extreme that they name: `checkpoint`: each population lies between 0.6 and 1.4 times its lattice weight.
All inputs are finite; a program needn't handle non-finite values. No bound on the sum of `wall_mask` on one device may be relied on, other than what follows from the above.
Results may differ from the reference program's by a relative error of at most 0.00009.
Values sent between devices are 32-bit elements; how exact they have to be, the bound alone decides.
A program may use at most 64 MiB of HBM per device.

```python
import math
import jax
import jax.numpy as jnp
import numpy as np
from jax import lax

NZ = 8
NX = 128
NY = 2048


def lattice_weights():
    signs = (-1, 0, 1)
    table = [8.0 / 27.0, 2.0 / 27.0, 1.0 / 54.0, 1.0 / 216.0]
    return [table[abs(a) + abs(b) + abs(c)] for a in signs for b in signs for c in signs]


def draw_checkpoint(key, part):
    weights = jnp.asarray(lattice_weights(), jnp.float32).reshape(27, 1, 1, 1)
    random_part = jax.random.uniform(key, (27, NZ, NX, NY), jnp.float32)
    factor = 0.6 + 0.8 * random_part
    return weights * factor


def with_ends(entries, rng, smallest, top_value):
    index_at = [jax.random.randint(jax.random.fold_in(rng, axis), (), 0, length) for axis, length in enumerate(entries.shape)]
    longest = entries.shape.index(max(entries.shape))
    neighbour = index_at[:longest] + [(index_at[longest] + 1) % entries.shape[longest]] + index_at[longest + 1:]
    return entries.at[tuple(index_at)].set(smallest).at[tuple(neighbour)].set(top_value)


def level_of(rng, extent, cuts, least, high):
    level = 1.0
    for dim, blocks in cuts:
        steps = jax.random.uniform(jax.random.fold_in(jax.random.fold_in(rng, 6), dim), (blocks,), jnp.float32, least / len(cuts), high / len(cuts))
        level = level * jnp.repeat(jnp.exp(steps), extent[dim] // blocks).reshape((-1,) + (1,) * (len(extent) - 1 - dim))
    return level


def noise(key, dims, deviation, limit, split=(), held_as=jnp.bfloat16):
    values = deviation * jax.random.normal(key, dims, jnp.float32)
    if split:
        values = values * level_of(key, dims, split, -0.22, 0.18)
    return jnp.clip(values, -limit, limit).astype(held_as)


def setup_inputs(seed: int = 0) -> dict:
    arg_keys = jax.random.split(jax.random.key(seed), 5)
    checkpoint = draw_checkpoint(jax.random.fold_in(arg_keys[4], 71), 0)
    rates = jnp.clip(jnp.exp(jax.random.uniform(arg_keys[1], (27,), jnp.float32, math.log(0.8), math.log(1.7))), 0.8, 1.7)
    wall_mask = with_ends((jax.random.randint(arg_keys[2], (NZ, NX, NY), 0, 6) < 1).astype(jnp.int32), jax.random.fold_in(arg_keys[2], 1), 0, 1)
    cotangent = noise(arg_keys[3], (27, NZ, NX, NY), 1.0, 6.0, ((2, 32), (3, 16)), jnp.float32)
    return dict(checkpoint=checkpoint, rates=rates, wall_mask=wall_mask, cotangent=cotangent)


def lattice_tables():
    signs = (-1, 0, 1)
    velocity = [[a, b, c] for a in signs for b in signs for c in signs]
    table = [8.0 / 27.0, 2.0 / 27.0, 1.0 / 54.0, 1.0 / 216.0]
    weights = [table[abs(a) + abs(b) + abs(c)] for a in signs for b in signs for c in signs]
    powers = [[1.0, 1.0, 1.0], [-1.0, 0.0, 1.0], [1.0, 0.0, 1.0]]
    undo = [[0.0, -0.5, 0.5], [1.0, 0.0, -1.0], [0.0, 0.5, 0.5]]
    moment = np.kron(np.kron(powers, powers), powers)
    inverse = np.kron(np.kron(undo, undo), undo)
    return (velocity, weights, moment, inverse)

def collide(incoming, rates, wall_cells):
    velocity, weights, moment, inverse = lattice_tables()
    velocity = jnp.asarray(velocity, jnp.float32)
    weights = jnp.asarray(weights, jnp.float32)
    moment = jnp.asarray(moment, jnp.float32)
    inverse = jnp.asarray(inverse, jnp.float32)
    high = lax.Precision.HIGHEST
    populations = incoming.reshape(27, -1)
    density = lax.optimization_barrier(jnp.sum(populations, axis=0))
    momentum = jnp.dot(velocity.T, populations, precision=high)
    speeds = momentum / density
    projected = jnp.dot(velocity, speeds, precision=high)
    speed_sq = lax.optimization_barrier(jnp.sum(speeds * speeds, axis=0))
    equilibrium = weights[:, None] * density * (1.0 + 3.0 * projected + 4.5 * projected * projected - 1.5 * speed_sq)
    relaxation = jnp.dot(inverse, rates[:, None] * moment, precision=high)
    collided = populations - jnp.dot(relaxation, populations - equilibrium, precision=high)
    reflected = populations[::-1]
    solid = wall_cells.reshape(1, -1)
    return (collided + solid * (reflected - collided)).reshape(incoming.shape)

def wall_field(wall_mask):
    height = lax.broadcasted_iota(jnp.int32, wall_mask.shape, 0)
    boundary = (height == 0) | (height == wall_mask.shape[0] - 1)
    return jnp.where(boundary, 1, wall_mask).astype(jnp.float32)

def stream(field, direction):
    pieces = []
    for slot in range(27):
        step_x = direction * (slot // 9 - 1)
        step_y = direction * (slot // 3 % 3 - 1)
        step_z = direction * (slot % 3 - 1)
        pieces.append(jnp.roll(field[slot], (step_z, step_x, step_y), axis=(0, 1, 2)))
    return jnp.stack(pieces)

def reference(checkpoint, rates, wall_mask, cotangent):
    wall_cells = wall_field(wall_mask)
    collided = collide(checkpoint, rates, wall_cells)
    next_state = stream(collided, 1)
    back_one = stream(cotangent, -1)
    _, pullback = jax.vjp(lambda value: collide(value, rates, wall_cells), next_state)
    grad_next = pullback(back_one)[0]
    back_two = stream(grad_next, -1)
    _, pullback_first = jax.vjp(lambda value: collide(value, rates, wall_cells), checkpoint)
    return pullback_first(back_two)[0]
```

```python
import functools

import jax
import jax.numpy as jnp
from jax import lax
from jax.experimental import pallas as pl
from jax.experimental.pallas import tpu as pltpu
from jax.sharding import PartitionSpec as P

F32 = jnp.float32
MESH = pl.DeviceIdType.MESH
ROWS = 4
Q = [(a, b, c) for a in (-1, 0, 1) for b in (-1, 0, 1) for c in (-1, 0, 1)]
THIRD = 1.0 / 3.0
NINTH = 1.0 / 9.0


def rollz(v, s):
    return v if s == 0 else pltpu.roll(v, s % 8, 0)


def rolly(v, s):
    return v if s % 128 == 0 else pltpu.roll(v, s % 128, 1)


def lanes():
    return lax.broadcasted_iota(jnp.int32, (8, 128), 1)


def along(values, axis, fn):
    out = [None] * 27
    step = (9, 3, 1)[axis]
    for i in range(27):
        if (i // step) % 3 == 0:
            out[i], out[i + step], out[i + 2 * step] = fn(
                values[i], values[i + step], values[i + 2 * step]
            )
    return out


def to_moments(a, b, c):
    s = a + c
    return s + b, c - a, s


def from_halved(m0, m1, m2):
    a, c = m2 - m1, m2 + m1
    return a, m0 - (a + c), c


def dual_doubled(a, b, c):
    return b, c - a, (a + c) - (b + b)


def dual_back(m0, m1, m2):
    s = m0 + m2
    return s - m1, m0, s + m1


def at(i, j, k):
    return 9 * i + 3 * j + k


def halved_rates(rates_ref):
    return [
        rates_ref[0, n] * (0.5 ** sum(p > 0 for p in (n // 9, n // 3 % 3, n % 3)))
        for n in range(27)
    ]


def collide(f, rates, wall):
    m = f
    for axis in (2, 1, 0):
        m = along(m, axis, to_moments)
    rho, jx, jy, jz = m[0], m[9], m[3], m[1]
    inv = 1.0 / rho
    ux, uy, uz = jx * inv, jy * inv, jz * inv
    xx, yy, zz = jx * ux, jy * uy, jz * uz
    xy, xz, yz = jx * uy, jx * uz, jy * uz
    r3, r9 = rho * THIRD, rho * NINTH
    x3, y3, z3 = jx * THIRD, jy * THIRD, jz * THIRD
    eq = [None] * 27
    eq[at(0, 0, 0)] = rho
    eq[at(1, 0, 0)], eq[at(0, 1, 0)], eq[at(0, 0, 1)] = jx, jy, jz
    eq[at(2, 0, 0)], eq[at(0, 2, 0)], eq[at(0, 0, 2)] = r3 + xx, r3 + yy, r3 + zz
    eq[at(1, 1, 0)], eq[at(1, 0, 1)], eq[at(0, 1, 1)] = xy, xz, yz
    eq[at(1, 2, 0)] = eq[at(1, 0, 2)] = x3
    eq[at(2, 1, 0)] = eq[at(0, 1, 2)] = y3
    eq[at(2, 0, 1)] = eq[at(0, 2, 1)] = z3
    eq[at(1, 2, 2)], eq[at(2, 1, 2)], eq[at(2, 2, 1)] = x3 * THIRD, y3 * THIRD, z3 * THIRD
    eq[at(1, 1, 2)], eq[at(1, 2, 1)], eq[at(2, 1, 1)] = xy * THIRD, xz * THIRD, yz * THIRD
    eq[at(2, 2, 0)] = r9 + (xx + yy) * THIRD
    eq[at(2, 0, 2)] = r9 + (xx + zz) * THIRD
    eq[at(0, 2, 2)] = r9 + (yy + zz) * THIRD
    eq[at(2, 2, 2)] = r9 * THIRD + (xx + yy + zz) * NINTH
    d = [
        m[n] * rates[n] if eq[n] is None else (m[n] - eq[n]) * rates[n]
        for n in range(27)
    ]
    for axis in (0, 1, 2):
        d = along(d, axis, from_halved)
    solid = wall > 0.5
    out = [jnp.where(solid, f[26 - n], f[n] - d[n]) for n in range(27)]
    return out, (ux, uy, uz)


def pull_back(g, u, rates, wall, keep=range(27)):
    ux, uy, uz = u
    e = g
    for axis in (2, 1, 0):
        e = along(e, axis, dual_doubled)
    e = [e[n] * rates[n] for n in range(27)]
    e222 = e[at(2, 2, 2)] * NINTH
    pair_xy, pair_xz, pair_yz = e[at(2, 2, 0)], e[at(2, 0, 2)], e[at(0, 2, 2)]
    pxx = e[at(2, 0, 0)] + (pair_xy + pair_xz) * THIRD + e222
    pyy = e[at(0, 2, 0)] + (pair_xy + pair_yz) * THIRD + e222
    pzz = e[at(0, 0, 2)] + (pair_xz + pair_yz) * THIRD + e222
    pxy = e[at(1, 1, 0)] + e[at(1, 1, 2)] * THIRD
    pxz = e[at(1, 0, 1)] + e[at(1, 2, 1)] * THIRD
    pyz = e[at(0, 1, 1)] + e[at(2, 1, 1)] * THIRD
    rho = (
        e[0]
        + (e[at(2, 0, 0)] + e[at(0, 2, 0)] + e[at(0, 0, 2)] + e222) * THIRD
        + (pair_xy + pair_xz + pair_yz) * NINTH
    )
    cx = e[at(1, 0, 0)] + (e[at(1, 2, 0)] + e[at(1, 0, 2)]) * THIRD + e[at(1, 2, 2)] * NINTH
    cy = e[at(0, 1, 0)] + (e[at(2, 1, 0)] + e[at(0, 1, 2)]) * THIRD + e[at(2, 1, 2)] * NINTH
    cz = e[at(0, 0, 1)] + (e[at(2, 0, 1)] + e[at(0, 2, 1)]) * THIRD + e[at(2, 2, 1)] * NINTH
    sx = (pxx + pxx) * ux + pxy * uy + pxz * uz
    sy = (pyy + pyy) * uy + pxy * ux + pyz * uz
    sz = (pzz + pzz) * uz + pxz * ux + pyz * uy
    rho = rho - 0.5 * (ux * sx + uy * sy + uz * sz)
    e[at(0, 0, 0)] = e[at(0, 0, 0)] - rho
    e[at(1, 0, 0)] = e[at(1, 0, 0)] - (cx + sx)
    e[at(0, 1, 0)] = e[at(0, 1, 0)] - (cy + sy)
    e[at(0, 0, 1)] = e[at(0, 0, 1)] - (cz + sz)
    for axis in (2, 1, 0):
        e = along(e, axis, dual_back)
    solid = wall > 0.5
    return {n: jnp.where(solid, g[26 - n], g[n] - e[n]) for n in keep}


def row(ref, q, x):
    return ref[pl.ds(q * 32 + x, 8, stride=4), :]


def wall_row(ref, x):
    height = lax.broadcasted_iota(jnp.int32, (8, 128), 0)
    mask = ref[pl.ds(x, 8, stride=4), :]
    return jnp.where((height == 0) | (height == 7), 1, mask).astype(F32)


def prepare(ck, cot, wall, rates_ref, sxc, mb, ey, uck):
    lane = lanes()
    rates = halved_rates(rates_ref)
    for q in range(18):
        sxc[1, q] = row(cot, q, 3)
        sxc[0, q] = row(cot, q + 9, 0)
    for q in range(9):
        sxc[1, 18 + q] = row(cot, q, 2)
        sxc[0, 18 + q] = row(cot, q + 18, 1)

    zero = jnp.zeros((8, 128), F32)
    first, last = lane == 0, lane == 127
    body = [[zero] * 4 for _ in range(6)]
    edge = [[zero] * 3 for _ in range(6)]
    for x in range(ROWS):
        w = wall_row(wall, x)
        mb[x + 1, 4] = w
        out, u = collide([row(ck, q, x) for q in range(27)], rates, w)
        for k in range(3):
            uck[x, k] = u[k]
        for a in range(3):
            sums, tilts = [], []
            for b in range(3):
                up = rollz(out[at(a, b, 2)], 1)
                down = rollz(out[at(a, b, 0)], -1)
                sums.append(out[at(a, b, 1)] + (up + down))
                tilts.append(up - down)
            ap, am = rolly(sums[2], 1), rolly(sums[0], -1)
            bp, bm = rolly(tilts[2], 1), rolly(tilts[0], -1)
            r = x + a
            outer = jnp.where(first, ap, am)
            edge[r][0] = edge[r][0] + outer
            edge[r][1] = edge[r][1] + (a - 1) * outer if a != 1 else edge[r][1]
            edge[r][2] = edge[r][2] + jnp.where(first, bp, bm)
            ap, am = jnp.where(first, 0.0, ap), jnp.where(last, 0.0, am)
            bp, bm = jnp.where(first, 0.0, bp), jnp.where(last, 0.0, bm)
            total = sums[1] + (ap + am)
            body[r][0] = body[r][0] + total
            if a != 1:
                body[r][1] = body[r][1] + (a - 1) * total
            body[r][2] = body[r][2] + (ap - am)
            body[r][3] = body[r][3] + (tilts[1] + (bp + bm))
    for r in range(6):
        for k in range(4):
            mb[r, k] = body[r][k]
    mb[0, 4] = zero
    mb[5, 4] = zero

    r0, r1, r2, l0, l1, l2, l0m = [zero] * 7
    for i, (cx, cz) in enumerate([(a, c) for a in range(3) for c in range(3)]):
        for x in range(ROWS):
            d = 8 * i + x + 2
            here, before, after = lane == d, lane == d - 1, lane == d + 1
            v = rolly(row(cot, at(cx, 0, cz), x), d - 127)
            r0, r2 = jnp.where(here, v, r0), jnp.where(before, v, r2)
            v = rolly(row(cot, at(cx, 2, cz), x), d)
            l0, l2 = jnp.where(here, v, l0), jnp.where(after, v, l2)
            v = rolly(row(cot, at(cx, 1, cz), x), d - 127)
            r1, l1 = jnp.where(here, v, r1), jnp.where(after, v, l1)
    for r in range(6):
        outer = edge[r]
        outer = [outer[0], outer[1], jnp.where(first, outer[0], -outer[0]), outer[2]]
        for k in range(4):
            d = 8 * (9 + k) + r + 1
            here, before, after = lane == d, lane == d - 1, lane == d + 1
            v = rolly(body[r][k], d - 127)
            r1, l1 = jnp.where(here, v, r1), jnp.where(after, v, l1)
            v = rolly(outer[k], d)
            r0, l0m = jnp.where(here, v, r0), jnp.where(before, v, l0m)
    for x in range(ROWS):
        d = 8 * 13 + x + 2
        v = rolly(wall_row(wall, x), d - 127)
        r1, l1 = jnp.where(lane == d, v, r1), jnp.where(lane == d + 1, v, l1)
    ey[0, 0] = l0 + rolly(l0m, 1)
    ey[1, 0] = rolly(l1, -1)
    ey[2, 0] = rolly(l2, -1)
    ey[0, 1] = r0
    ey[1, 1] = r1
    ey[2, 1] = rolly(r2, 1)


def exchange(sizes, sxc, mb, ey, xc, xm, xe, en, send, recv):
    nx, ny = sizes

    def device(dx, dy):
        return (
            lax.rem(lax.axis_index("gx") + (dx + nx), nx),
            lax.rem(lax.axis_index("gy") + (dy + ny), ny),
        )

    around = [(a, b) for a in (1, 0, -1) for b in (1, 0, -1) if (a, b) != (0, 0)]
    barrier = pltpu.get_barrier_semaphore()
    for d in around:
        pl.semaphore_signal(barrier, inc=1, device_id=device(*d), device_id_type=MESH)
    pl.semaphore_wait(barrier, 8)
    copies = []

    def put(src, dst, dx, dy):
        n = len(copies)
        copies.append(
            pltpu.make_async_remote_copy(
                src_ref=src,
                dst_ref=dst,
                send_sem=send.at[n],
                recv_sem=recv.at[n],
                device_id=device(dx, dy),
                device_id_type=MESH,
            )
        )
        copies[-1].start()

    put(ey.at[:, 1], en.at[1], 1, 1)
    put(ey.at[:, 0], en.at[4], 1, -1)
    put(mb.at[pl.ds(4, 2)], xm.at[0], 1, 0)
    put(ey.at[0], xe.at[0], 1, 0)
    put(sxc.at[1], xc.at[0], 1, 0)
    put(ey.at[:, 1], en.at[2], -1, 1)
    put(ey.at[:, 0], en.at[5], -1, -1)
    put(mb.at[pl.ds(0, 2)], xm.at[1], -1, 0)
    put(ey.at[0], xe.at[1], -1, 0)
    put(sxc.at[0], xc.at[1], -1, 0)
    put(ey.at[:, 1], en.at[0], 0, 1)
    put(ey.at[:, 0], en.at[3], 0, -1)
    for c in copies:
        c.wait_recv()
    for c in copies:
        c.wait_send()


def finish(cot, wall, rates_ref, mb, ey, uck, xc, xm, xe, en, out, gn, gy):
    lane = lanes()
    rates = halved_rates(rates_ref)
    first, last = lane == 0, lane == 127
    low, high = lane % 8 < 3, lane % 8 >= 5
    left = lane < 8

    def merge(own, below, above):
        below, above = rolly(below, -4), rolly(above, 4)
        return own + jnp.where(low, below, 0.0) + jnp.where(high, above, 0.0)

    exl = [merge(en[0, k], en[1, k], en[2, k]) for k in range(3)]
    exr = [merge(en[3, k], en[4, k], en[5, k]) for k in range(3)]
    oxl = merge(ey[0, 0], xe[0, 0], xe[1, 0])
    oxr = merge(ey[0, 1], xe[0, 1], xe[1, 1])

    def source(q, x):
        if 0 <= x < ROWS:
            return row(cot, q, x)
        if x == -1:
            return xc[0, q]
        if x == -2:
            return xc[0, 18 + q]
        return xc[1, q - 9] if x == ROWS else xc[1, q]

    def slot(q):
        return 3 * (q // 9) + q % 3

    g = []
    for q, (cx, cy, cz) in enumerate(Q):
        s = slot(q)
        lo, hi = ((exl[2], oxr), (exl[1], exr[1]), (oxl, exr[2]))[cy + 1]
        v = jnp.where(left, rolly(lo, -8 * s - cx), rolly(hi, 8 - 8 * s - cx))
        g.append(rollz(v, -cz))
    m = []
    for k in range(4):
        s = 9 + k
        lo, hi = exl[1] + oxl, exr[1] + oxr
        m.append(jnp.where(left, rolly(lo, -8 * s), rolly(hi, 8 - 8 * s)))
    w = jnp.where(left, rolly(exl[1], -104), rolly(exr[1], -96))
    inv = 1.0 / jnp.where((lane < 16) & (lane % 8 > 0) & (lane % 8 < 7), m[0], 1.0)
    got = pull_back(g, [m[k] * inv for k in (1, 2, 3)], rates, w)
    for q, (cx, cy, cz) in enumerate(Q):
        if cy != 0:
            gy[q] = got[q]

    for x in range(-1, ROWS + 1):
        m = []
        for k in range(4):
            v = mb[x + 1, k]
            if x <= 0:
                v = v + xm[0, x + 1, k]
            if x >= 3:
                v = v + xm[1, x - 3, k]
            d = 8 * (9 + k) + x + 2
            v = v + jnp.where(first, rolly(exl[0], -d), 0.0)
            v = v + jnp.where(last, rolly(exr[0], 127 - d), 0.0)
            m.append(v)
        w = xm[0, 0, 4] if x < 0 else xm[1, 1, 4] if x == ROWS else wall_row(wall, x)
        g = []
        for q, (cx, cy, cz) in enumerate(Q):
            v = source(q, x + cx)
            d = 8 * slot(q) + x + cx + 2
            if cy == 1:
                v = jnp.where(last, rolly(exr[0], 127 - d), rolly(v, -1))
            if cy == -1:
                v = jnp.where(first, rolly(exl[0], -d), rolly(v, 1))
            g.append(rollz(v, -cz))
        inv = 1.0 / m[0]
        keep = range(9) if x < 0 else range(18, 27) if x == ROWS else range(27)
        got = pull_back(g, [m[k] * inv for k in (1, 2, 3)], rates, w, keep)
        for q in keep:
            gn[x + 1, q] = got[q]

    for x in range(ROWS):
        g = []
        for q, (cx, cy, cz) in enumerate(Q):
            v = gn[x + cx + 1, q]
            d = x + cx + 2
            if cy == 1:
                v = jnp.where(last, rolly(gy[q], 127 - 8 - d), rolly(v, -1))
            if cy == -1:
                v = jnp.where(first, rolly(gy[q], -d), rolly(v, 1))
            g.append(rollz(v, -cz))
        got = pull_back(g, [uck[x, k] for k in range(3)], rates, wall_row(wall, x))
        for q in range(27):
            out[pl.ds(q * 32 + x, 8, stride=4), :] = got[q]


def shards(sizes, checkpoint, rates, wall_mask, cotangent):
    ck, cot = checkpoint.reshape(864, 128), cotangent.reshape(864, 128)
    wall, rates = wall_mask.reshape(32, 128), rates.reshape(1, 27)
    vmem, smem = pl.BlockSpec(memory_space=pltpu.VMEM), pl.BlockSpec(memory_space=pltpu.SMEM)
    small = dict(vmem_limit_bytes=16 << 20)

    def like(*shape):
        return jax.ShapeDtypeStruct(shape, F32)

    sxc, mb, ey, uck = pl.pallas_call(
        prepare,
        out_shape=(like(2, 27, 8, 128), like(6, 5, 8, 128), like(3, 2, 8, 128), like(4, 3, 8, 128)),
        in_specs=[vmem, vmem, vmem, smem],
        out_specs=(vmem,) * 4,
        compiler_params=pltpu.CompilerParams(**small),
        name="prepare",
    )(ck, cot, wall, rates)
    xc, xm, xe, en = pl.pallas_call(
        functools.partial(exchange, sizes),
        out_shape=(like(2, 27, 8, 128), like(2, 2, 5, 8, 128), like(2, 2, 8, 128), like(6, 3, 8, 128)),
        in_specs=[vmem] * 3,
        out_specs=(vmem,) * 4,
        scratch_shapes=[pltpu.SemaphoreType.DMA((12,)), pltpu.SemaphoreType.DMA((12,))],
        compiler_params=pltpu.CompilerParams(collective_id=0, has_side_effects=True, **small),
        name="exchange",
    )(sxc, mb, ey)
    grad = pl.pallas_call(
        finish,
        out_shape=like(864, 128),
        in_specs=[vmem, vmem, smem] + [vmem] * 7,
        out_specs=vmem,
        scratch_shapes=[pltpu.VMEM((6, 27, 8, 128), F32), pltpu.VMEM((27, 8, 128), F32)],
        compiler_params=pltpu.CompilerParams(**small),
        name="finish",
    )(cot, wall, rates, mb, ey, uck, xc, xm, xe, en)
    return grad.reshape(checkpoint.shape)


def solution(mesh):
    sizes = (mesh.shape["gx"], mesh.shape["gy"])
    in_specs = (P(None, None, "gx", "gy"), P(), P(None, "gx", "gy"), P(None, None, "gx", "gy"))
    out_specs = P(None, None, "gx", "gy")
    return jax.shard_map(
        functools.partial(shards, sizes), mesh=mesh, in_specs=in_specs, out_specs=out_specs, check_vma=False
    )
```

```python
import functools

import jax
import jax.numpy as jnp
from jax import lax
from jax.experimental import pallas as pl
from jax.experimental.pallas import tpu as pltpu
from jax.sharding import PartitionSpec as P

F32 = jnp.float32
MESH = pl.DeviceIdType.MESH
ROWS = 4
Q = [(a, b, c) for a in (-1, 0, 1) for b in (-1, 0, 1) for c in (-1, 0, 1)]
THIRD = 1.0 / 3.0
NINTH = 1.0 / 9.0


def rollz(v, s):
    return v if s == 0 else pltpu.roll(v, s % 8, 0)


def rolly(v, s):
    return v if s % 128 == 0 else pltpu.roll(v, s % 128, 1)


def lanes():
    return lax.broadcasted_iota(jnp.int32, (8, 128), 1)


def along(values, axis, fn):
    out = [None] * 27
    step = (9, 3, 1)[axis]
    for i in range(27):
        if (i // step) % 3 == 0:
            out[i], out[i + step], out[i + 2 * step] = fn(
                values[i], values[i + step], values[i + 2 * step]
            )
    return out


def to_moments(a, b, c):
    s = a + c
    return s + b, c - a, s


def from_halved(m0, m1, m2):
    a, c = m2 - m1, m2 + m1
    return a, m0 - (a + c), c


def dual_doubled(a, b, c):
    return b, c - a, (a + c) - (b + b)


def dual_back(m0, m1, m2):
    s = m0 + m2
    return s - m1, m0, s + m1


def at(i, j, k):
    return 9 * i + 3 * j + k


def halved_rates(rates_ref):
    return [
        rates_ref[0, n] * (0.5 ** sum(p > 0 for p in (n // 9, n // 3 % 3, n % 3)))
        for n in range(27)
    ]


def collide(f, rates, wall):
    m = f
    for axis in (2, 1, 0):
        m = along(m, axis, to_moments)
    rho, jx, jy, jz = m[0], m[9], m[3], m[1]
    inv = 1.0 / rho
    ux, uy, uz = jx * inv, jy * inv, jz * inv
    xx, yy, zz = jx * ux, jy * uy, jz * uz
    xy, xz, yz = jx * uy, jx * uz, jy * uz
    r3, r9 = rho * THIRD, rho * NINTH
    x3, y3, z3 = jx * THIRD, jy * THIRD, jz * THIRD
    eq = [None] * 27
    eq[at(0, 0, 0)] = rho
    eq[at(1, 0, 0)], eq[at(0, 1, 0)], eq[at(0, 0, 1)] = jx, jy, jz
    eq[at(2, 0, 0)], eq[at(0, 2, 0)], eq[at(0, 0, 2)] = r3 + xx, r3 + yy, r3 + zz
    eq[at(1, 1, 0)], eq[at(1, 0, 1)], eq[at(0, 1, 1)] = xy, xz, yz
    eq[at(1, 2, 0)] = eq[at(1, 0, 2)] = x3
    eq[at(2, 1, 0)] = eq[at(0, 1, 2)] = y3
    eq[at(2, 0, 1)] = eq[at(0, 2, 1)] = z3
    eq[at(1, 2, 2)], eq[at(2, 1, 2)], eq[at(2, 2, 1)] = x3 * THIRD, y3 * THIRD, z3 * THIRD
    eq[at(1, 1, 2)], eq[at(1, 2, 1)], eq[at(2, 1, 1)] = xy * THIRD, xz * THIRD, yz * THIRD
    eq[at(2, 2, 0)] = r9 + (xx + yy) * THIRD
    eq[at(2, 0, 2)] = r9 + (xx + zz) * THIRD
    eq[at(0, 2, 2)] = r9 + (yy + zz) * THIRD
    eq[at(2, 2, 2)] = r9 * THIRD + (xx + yy + zz) * NINTH
    d = [
        m[n] * rates[n] if eq[n] is None else (m[n] - eq[n]) * rates[n]
        for n in range(27)
    ]
    for axis in (0, 1, 2):
        d = along(d, axis, from_halved)
    solid = wall > 0.5
    out = [jnp.where(solid, f[26 - n], f[n] - d[n]) for n in range(27)]
    return out, (ux, uy, uz)


def pull_back(g, u, rates, wall, keep=range(27)):
    ux, uy, uz = u
    e = g
    for axis in (2, 1, 0):
        e = along(e, axis, dual_doubled)
    e = [e[n] * rates(n) for n in range(27)]
    e222 = e[at(2, 2, 2)] * NINTH
    pair_xy, pair_xz, pair_yz = e[at(2, 2, 0)], e[at(2, 0, 2)], e[at(0, 2, 2)]
    pxx = e[at(2, 0, 0)] + (pair_xy + pair_xz) * THIRD + e222
    pyy = e[at(0, 2, 0)] + (pair_xy + pair_yz) * THIRD + e222
    pzz = e[at(0, 0, 2)] + (pair_xz + pair_yz) * THIRD + e222
    pxy = e[at(1, 1, 0)] + e[at(1, 1, 2)] * THIRD
    pxz = e[at(1, 0, 1)] + e[at(1, 2, 1)] * THIRD
    pyz = e[at(0, 1, 1)] + e[at(2, 1, 1)] * THIRD
    rho = (
        e[0]
        + (e[at(2, 0, 0)] + e[at(0, 2, 0)] + e[at(0, 0, 2)] + e222) * THIRD
        + (pair_xy + pair_xz + pair_yz) * NINTH
    )
    cx = e[at(1, 0, 0)] + (e[at(1, 2, 0)] + e[at(1, 0, 2)]) * THIRD + e[at(1, 2, 2)] * NINTH
    cy = e[at(0, 1, 0)] + (e[at(2, 1, 0)] + e[at(0, 1, 2)]) * THIRD + e[at(2, 1, 2)] * NINTH
    cz = e[at(0, 0, 1)] + (e[at(2, 0, 1)] + e[at(0, 2, 1)]) * THIRD + e[at(2, 2, 1)] * NINTH
    sx = (pxx + pxx) * ux + pxy * uy + pxz * uz
    sy = (pyy + pyy) * uy + pxy * ux + pyz * uz
    sz = (pzz + pzz) * uz + pxz * ux + pyz * uy
    rho = rho - 0.5 * (ux * sx + uy * sy + uz * sz)
    e[at(0, 0, 0)] = e[at(0, 0, 0)] - rho
    e[at(1, 0, 0)] = e[at(1, 0, 0)] - (cx + sx)
    e[at(0, 1, 0)] = e[at(0, 1, 0)] - (cy + sy)
    e[at(0, 0, 1)] = e[at(0, 0, 1)] - (cz + sz)
    for axis in (2, 1, 0):
        e = along(e, axis, dual_back)
    solid = wall > 0.5
    return {n: jnp.where(solid, g[26 - n], g[n] - e[n]) for n in keep}


def row(ref, q, x):
    return ref[pl.ds(q * 32 + x, 8, stride=4), :]


def wall_row(ref, x):
    height = lax.broadcasted_iota(jnp.int32, (8, 128), 0)
    mask = ref[pl.ds(x, 8, stride=4), :]
    return jnp.where((height == 0) | (height == 7), 1, mask).astype(F32)


def exchange(
    sizes, ck_hbm, cot_hbm, wall_hbm, rates_hbm,
    cot, mb, ey, uck, rv, xc, xm, xe, en,
    ck, wall, rates_ref, sxc, ehi, load, ready, send, recv,
):
    nx, ny = sizes
    lane = lanes()

    def device(dx, dy):
        return (
            lax.rem(lax.axis_index("gx") + (dx + nx), nx),
            lax.rem(lax.axis_index("gy") + (dy + ny), ny),
        )

    def signal(sem, dx):
        for dy in (0, 1, -1):
            pl.semaphore_signal(sem, inc=1, device_id=device(dx, dy), device_id_type=MESH)

    barrier = pltpu.get_barrier_semaphore()
    signal(barrier, -1)
    loads = []
    for src, dst in ((cot_hbm, cot), (ck_hbm, ck), (wall_hbm, wall), (rates_hbm, rates_ref)):
        loads.append(pltpu.make_async_copy(src, dst, load.at[len(loads)]))
        loads[-1].start()
    pl.semaphore_wait(barrier, 3)
    signal(ready, 1)

    copies = []

    def put(src, dst, dx, dy):
        n = len(copies)
        copies.append(
            pltpu.make_async_remote_copy(
                src_ref=src,
                dst_ref=dst,
                send_sem=send.at[n],
                recv_sem=recv.at[n],
                device_id=device(dx, dy),
                device_id_type=MESH,
            )
        )
        copies[-1].start()

    loads[0].wait()
    for q in range(18):
        sxc[1, q] = row(cot, q, 3)
    for q in range(9):
        sxc[1, 18 + q] = row(cot, q, 2)
    put(sxc.at[1], xc.at[0], 1, 0)
    for q in range(18):
        sxc[0, q] = row(cot, q + 9, 0)
    for q in range(9):
        sxc[0, 18 + q] = row(cot, q + 18, 1)

    zero = jnp.zeros((8, 128), F32)
    first, last = lane == 0, lane == 127
    body = [[zero] * 4 for _ in range(6)]
    edge = [[zero] * 3 for _ in range(6)]
    acc = dict.fromkeys(("r0", "r1", "r2", "l0", "l1", "l2", "l0m"), zero)

    def add(name, v, d):
        acc[name] = jnp.where(lane == d, v, acc[name])

    def pack_cotangent(x):
        for i, (cx, cz) in enumerate([(a, c) for a in range(3) for c in range(3)]):
            d = 8 * i + x + 2
            v = rolly(row(cot, at(cx, 0, cz), x), d - 127)
            add("r0", v, d)
            add("r2", v, d - 1)
            v = rolly(row(cot, at(cx, 2, cz), x), d)
            add("l0", v, d)
            add("l2", v, d + 1)
            v = rolly(row(cot, at(cx, 1, cz), x), d - 127)
            add("r1", v, d)
            add("l1", v, d + 1)

    def pack_sums(r):
        outer = edge[r]
        outer = [outer[0], outer[1], jnp.where(first, outer[0], -outer[0]), outer[2]]
        for k in range(4):
            d = 8 * (9 + k) + r + 1
            v = rolly(body[r][k], d - 127)
            add("r1", v, d)
            add("l1", v, d + 1)
            v = rolly(outer[k], d)
            add("r0", v, d)
            add("l0m", v, d - 1)

    def pack_wall(x, w):
        d = 8 * 13 + x + 2
        v = rolly(w, d - 127)
        add("r1", v, d)
        add("l1", v, d + 1)

    def store_packs(ref):
        ref[0, 0] = acc["l0"] + rolly(acc["l0m"], 1)
        ref[1, 0] = rolly(acc["l1"], -1)
        ref[2, 0] = rolly(acc["l2"], -1)
        ref[0, 1] = acc["r0"]
        ref[1, 1] = acc["r1"]
        ref[2, 1] = rolly(acc["r2"], 1)

    def collide_row(x):
        w = wall_row(wall, x)
        mb[x + 1, 4] = w
        pack_wall(x, w)
        out, u = collide([row(ck, q, x) for q in range(27)], rates, w)
        for k in range(3):
            uck[x, k] = u[k]
        for a in range(3):
            sums, tilts = [], []
            for b in range(3):
                up = rollz(out[at(a, b, 2)], 1)
                down = rollz(out[at(a, b, 0)], -1)
                sums.append(out[at(a, b, 1)] + (up + down))
                tilts.append(up - down)
            ap, am = rolly(sums[2], 1), rolly(sums[0], -1)
            bp, bm = rolly(tilts[2], 1), rolly(tilts[0], -1)
            r = x + a
            outer = jnp.where(first, ap, am)
            edge[r][0] = edge[r][0] + outer
            edge[r][1] = edge[r][1] + (a - 1) * outer if a != 1 else edge[r][1]
            edge[r][2] = edge[r][2] + jnp.where(first, bp, bm)
            ap, am = jnp.where(first, 0.0, ap), jnp.where(last, 0.0, am)
            bp, bm = jnp.where(first, 0.0, bp), jnp.where(last, 0.0, bm)
            total = sums[1] + (ap + am)
            body[r][0] = body[r][0] + total
            if a != 1:
                body[r][1] = body[r][1] + (a - 1) * total
            body[r][2] = body[r][2] + (ap - am)
            body[r][3] = body[r][3] + (tilts[1] + (bp + bm))

    def store_sums(r):
        for k in range(4):
            mb[r, k] = body[r][k]
        pack_sums(r)

    pack_cotangent(3)
    pack_cotangent(2)
    for c in loads[1:]:
        c.wait()
    rates = halved_rates(rates_ref)
    mb[5, 4] = zero
    collide_row(3)
    collide_row(2)
    store_sums(5)
    store_sums(4)
    store_packs(ehi)
    put(ehi.at[:, 1], en.at[1], 1, 1)
    put(ehi.at[:, 0], en.at[4], 1, -1)
    put(mb.at[pl.ds(4, 2)], xm.at[0], 1, 0)
    put(ehi.at[0], xe.at[0], 1, 0)

    mb[0, 4] = zero
    pack_cotangent(1)
    pack_cotangent(0)
    collide_row(1)
    collide_row(0)
    for r in range(4):
        store_sums(r)
    store_packs(ey)
    pl.semaphore_wait(ready, 3)
    put(sxc.at[0], xc.at[1], -1, 0)
    put(ey.at[:, 1], en.at[2], -1, 1)
    put(ey.at[:, 0], en.at[5], -1, -1)
    put(mb.at[pl.ds(0, 2)], xm.at[1], -1, 0)
    put(ey.at[0], xe.at[1], -1, 0)
    put(ey.at[:, 1], en.at[0], 0, 1)
    put(ey.at[:, 0], en.at[3], 0, -1)
    for n in range(27):
        rv[n] = jnp.full((8, 128), rates[n], F32)
    for c in copies:
        c.wait_recv()
    for c in copies:
        c.wait_send()


def finish(cot, mb, ey, uck, rv, xc, xm, xe, en, out, gn, gy):
    lane = lanes()

    def rates(n):
        return rv[n]

    first, last = lane == 0, lane == 127
    low, high = lane % 8 < 3, lane % 8 >= 5
    left = lane < 8

    def merge(own, below, above):
        below, above = rolly(below, -4), rolly(above, 4)
        return own + jnp.where(low, below, 0.0) + jnp.where(high, above, 0.0)

    exl = [merge(en[0, k], en[1, k], en[2, k]) for k in range(3)]
    exr = [merge(en[3, k], en[4, k], en[5, k]) for k in range(3)]
    oxl = merge(ey[0, 0], xe[0, 0], xe[1, 0])
    oxr = merge(ey[0, 1], xe[0, 1], xe[1, 1])

    def source(q, x):
        if 0 <= x < ROWS:
            return row(cot, q, x)
        if x == -1:
            return xc[0, q]
        if x == -2:
            return xc[0, 18 + q]
        return xc[1, q - 9] if x == ROWS else xc[1, q]

    def slot(q):
        return 3 * (q // 9) + q % 3

    g = []
    for q, (cx, cy, cz) in enumerate(Q):
        s = slot(q)
        lo, hi = ((exl[2], oxr), (exl[1], exr[1]), (oxl, exr[2]))[cy + 1]
        v = jnp.where(left, rolly(lo, -8 * s - cx), rolly(hi, 8 - 8 * s - cx))
        g.append(rollz(v, -cz))
    m = []
    for k in range(4):
        s = 9 + k
        lo, hi = exl[1] + oxl, exr[1] + oxr
        m.append(jnp.where(left, rolly(lo, -8 * s), rolly(hi, 8 - 8 * s)))
    w = jnp.where(left, rolly(exl[1], -104), rolly(exr[1], -96))
    inv = 1.0 / jnp.where((lane < 16) & (lane % 8 > 0) & (lane % 8 < 7), m[0], 1.0)
    got = pull_back(g, [m[k] * inv for k in (1, 2, 3)], rates, w)
    for q, (cx, cy, cz) in enumerate(Q):
        if cy != 0:
            gy[q] = got[q]

    for x in range(-1, ROWS + 1):
        m = []
        for k in range(4):
            v = mb[x + 1, k]
            if x <= 0:
                v = v + xm[0, x + 1, k]
            if x >= 3:
                v = v + xm[1, x - 3, k]
            d = 8 * (9 + k) + x + 2
            v = v + jnp.where(first, rolly(exl[0], -d), 0.0)
            v = v + jnp.where(last, rolly(exr[0], 127 - d), 0.0)
            m.append(v)
        w = xm[0, 0, 4] if x < 0 else xm[1, 1, 4] if x == ROWS else mb[x + 1, 4]
        g = []
        for q, (cx, cy, cz) in enumerate(Q):
            v = source(q, x + cx)
            d = 8 * slot(q) + x + cx + 2
            if cy == 1:
                v = jnp.where(last, rolly(exr[0], 127 - d), rolly(v, -1))
            if cy == -1:
                v = jnp.where(first, rolly(exl[0], -d), rolly(v, 1))
            g.append(rollz(v, -cz))
        inv = 1.0 / m[0]
        keep = range(9) if x < 0 else range(18, 27) if x == ROWS else range(27)
        got = pull_back(g, [m[k] * inv for k in (1, 2, 3)], rates, w, keep)
        for q in keep:
            gn[x + 1, q] = got[q]

    for x in range(ROWS):
        g = []
        for q, (cx, cy, cz) in enumerate(Q):
            v = gn[x + cx + 1, q]
            d = x + cx + 2
            if cy == 1:
                v = jnp.where(last, rolly(gy[q], 127 - 8 - d), rolly(v, -1))
            if cy == -1:
                v = jnp.where(first, rolly(gy[q], -d), rolly(v, 1))
            g.append(rollz(v, -cz))
        got = pull_back(g, [uck[x, k] for k in range(3)], rates, mb[x + 1, 4])
        for q in range(27):
            out[pl.ds(q * 32 + x, 8, stride=4), :] = got[q]


def shards(sizes, checkpoint, rates, wall_mask, cotangent):
    ck, cot = checkpoint.reshape(864, 128), cotangent.reshape(864, 128)
    wall, rates = wall_mask.reshape(32, 128), rates.reshape(1, 27)
    vmem, hbm = pl.BlockSpec(memory_space=pltpu.VMEM), pl.BlockSpec(memory_space=pltpu.HBM)
    small = dict(vmem_limit_bytes=16 << 20)

    def like(*shape):
        return jax.ShapeDtypeStruct(shape, F32)

    got = pl.pallas_call(
        functools.partial(exchange, sizes),
        out_shape=(
            like(864, 128), like(6, 5, 8, 128), like(3, 2, 8, 128), like(4, 3, 8, 128), like(27, 8, 128),
            like(2, 27, 8, 128), like(2, 2, 5, 8, 128), like(2, 2, 8, 128), like(6, 3, 8, 128),
        ),
        in_specs=[hbm] * 4,
        out_specs=(vmem,) * 9,
        scratch_shapes=[
            pltpu.VMEM((864, 128), F32),
            pltpu.VMEM((32, 128), jnp.int32),
            pltpu.SMEM((1, 27), F32),
            pltpu.VMEM((2, 27, 8, 128), F32),
            pltpu.VMEM((3, 2, 8, 128), F32),
            pltpu.SemaphoreType.DMA((4,)),
            pltpu.SemaphoreType.REGULAR,
            pltpu.SemaphoreType.DMA((12,)),
            pltpu.SemaphoreType.DMA((12,)),
        ],
        compiler_params=pltpu.CompilerParams(collective_id=0, has_side_effects=True, **small),
        name="exchange",
    )(*[pltpu.with_memory_space_constraint(v, pltpu.HBM) for v in (ck, cot, wall, rates)])
    grad = pl.pallas_call(
        finish,
        out_shape=like(864, 128),
        in_specs=[vmem] * 9,
        out_specs=vmem,
        scratch_shapes=[pltpu.VMEM((6, 27, 8, 128), F32), pltpu.VMEM((27, 8, 128), F32)],
        compiler_params=pltpu.CompilerParams(**small),
        name="finish",
    )(*got)
    return grad.reshape(checkpoint.shape)


def solution(mesh):
    sizes = (mesh.shape["gx"], mesh.shape["gy"])
    in_specs = (P(None, None, "gx", "gy"), P(), P(None, "gx", "gy"), P(None, None, "gx", "gy"))
    out_specs = P(None, None, "gx", "gy")
    return jax.shard_map(
        functools.partial(shards, sizes), mesh=mesh, in_specs=in_specs, out_specs=out_specs, check_vma=False
    )
```

```python
import functools

import jax
import jax.numpy as jnp
from jax import lax
from jax.experimental import pallas as pl
from jax.experimental.pallas import tpu as pltpu
from jax.sharding import PartitionSpec as P

F32 = jnp.float32
MESH = pl.DeviceIdType.MESH
ROWS = 4
Q = [(a, b, c) for a in (-1, 0, 1) for b in (-1, 0, 1) for c in (-1, 0, 1)]
THIRD = 1.0 / 3.0
NINTH = 1.0 / 9.0


def rollz(v, s):
    return v if s == 0 else pltpu.roll(v, s % 8, 0)


def rolly(v, s):
    return v if s % 128 == 0 else pltpu.roll(v, s % 128, 1)


def lanes():
    return lax.broadcasted_iota(jnp.int32, (8, 128), 1)


def along(values, axis, fn):
    out = [None] * 27
    step = (9, 3, 1)[axis]
    for i in range(27):
        if (i // step) % 3 == 0:
            out[i], out[i + step], out[i + 2 * step] = fn(
                values[i], values[i + step], values[i + 2 * step]
            )
    return out


def to_moments(a, b, c):
    s = a + c
    return s + b, c - a, s


def from_halved(m0, m1, m2):
    a, c = m2 - m1, m2 + m1
    return a, m0 - (a + c), c


def dual_doubled(a, b, c):
    return b, c - a, (a + c) - (b + b)


def dual_back(m0, m1, m2):
    s = m0 + m2
    return s - m1, m0, s + m1


def at(i, j, k):
    return 9 * i + 3 * j + k


def halved_rates(rates_ref):
    return [
        rates_ref[0, n] * (0.5 ** sum(p > 0 for p in (n // 9, n // 3 % 3, n % 3)))
        for n in range(27)
    ]


def collide(f, rates, wall):
    m = f
    for axis in (2, 1, 0):
        m = along(m, axis, to_moments)
    rho, jx, jy, jz = m[0], m[9], m[3], m[1]
    inv = 1.0 / rho
    ux, uy, uz = jx * inv, jy * inv, jz * inv
    xx, yy, zz = jx * ux, jy * uy, jz * uz
    xy, xz, yz = jx * uy, jx * uz, jy * uz
    r3, r9 = rho * THIRD, rho * NINTH
    x3, y3, z3 = jx * THIRD, jy * THIRD, jz * THIRD
    eq = [None] * 27
    eq[at(0, 0, 0)] = rho
    eq[at(1, 0, 0)], eq[at(0, 1, 0)], eq[at(0, 0, 1)] = jx, jy, jz
    eq[at(2, 0, 0)], eq[at(0, 2, 0)], eq[at(0, 0, 2)] = r3 + xx, r3 + yy, r3 + zz
    eq[at(1, 1, 0)], eq[at(1, 0, 1)], eq[at(0, 1, 1)] = xy, xz, yz
    eq[at(1, 2, 0)] = eq[at(1, 0, 2)] = x3
    eq[at(2, 1, 0)] = eq[at(0, 1, 2)] = y3
    eq[at(2, 0, 1)] = eq[at(0, 2, 1)] = z3
    eq[at(1, 2, 2)], eq[at(2, 1, 2)], eq[at(2, 2, 1)] = x3 * THIRD, y3 * THIRD, z3 * THIRD
    eq[at(1, 1, 2)], eq[at(1, 2, 1)], eq[at(2, 1, 1)] = xy * THIRD, xz * THIRD, yz * THIRD
    eq[at(2, 2, 0)] = r9 + (xx + yy) * THIRD
    eq[at(2, 0, 2)] = r9 + (xx + zz) * THIRD
    eq[at(0, 2, 2)] = r9 + (yy + zz) * THIRD
    eq[at(2, 2, 2)] = r9 * THIRD + (xx + yy + zz) * NINTH
    d = [
        m[n] * rates[n] if eq[n] is None else (m[n] - eq[n]) * rates[n]
        for n in range(27)
    ]
    for axis in (0, 1, 2):
        d = along(d, axis, from_halved)
    solid = wall > 0.5
    out = [jnp.where(solid, f[26 - n], f[n] - d[n]) for n in range(27)]
    return out, (ux, uy, uz)


def pull_back(g, u, rates, wall, keep=range(27)):
    ux, uy, uz = u
    e = g
    for axis in (2, 1, 0):
        e = along(e, axis, dual_doubled)
    e = [e[n] * rates(n) for n in range(27)]
    e222 = e[at(2, 2, 2)] * NINTH
    pair_xy, pair_xz, pair_yz = e[at(2, 2, 0)], e[at(2, 0, 2)], e[at(0, 2, 2)]
    pxx = e[at(2, 0, 0)] + (pair_xy + pair_xz) * THIRD + e222
    pyy = e[at(0, 2, 0)] + (pair_xy + pair_yz) * THIRD + e222
    pzz = e[at(0, 0, 2)] + (pair_xz + pair_yz) * THIRD + e222
    pxy = e[at(1, 1, 0)] + e[at(1, 1, 2)] * THIRD
    pxz = e[at(1, 0, 1)] + e[at(1, 2, 1)] * THIRD
    pyz = e[at(0, 1, 1)] + e[at(2, 1, 1)] * THIRD
    rho = (
        e[0]
        + (e[at(2, 0, 0)] + e[at(0, 2, 0)] + e[at(0, 0, 2)] + e222) * THIRD
        + (pair_xy + pair_xz + pair_yz) * NINTH
    )
    cx = e[at(1, 0, 0)] + (e[at(1, 2, 0)] + e[at(1, 0, 2)]) * THIRD + e[at(1, 2, 2)] * NINTH
    cy = e[at(0, 1, 0)] + (e[at(2, 1, 0)] + e[at(0, 1, 2)]) * THIRD + e[at(2, 1, 2)] * NINTH
    cz = e[at(0, 0, 1)] + (e[at(2, 0, 1)] + e[at(0, 2, 1)]) * THIRD + e[at(2, 2, 1)] * NINTH
    sx = (pxx + pxx) * ux + pxy * uy + pxz * uz
    sy = (pyy + pyy) * uy + pxy * ux + pyz * uz
    sz = (pzz + pzz) * uz + pxz * ux + pyz * uy
    rho = rho - 0.5 * (ux * sx + uy * sy + uz * sz)
    e[at(0, 0, 0)] = e[at(0, 0, 0)] - rho
    e[at(1, 0, 0)] = e[at(1, 0, 0)] - (cx + sx)
    e[at(0, 1, 0)] = e[at(0, 1, 0)] - (cy + sy)
    e[at(0, 0, 1)] = e[at(0, 0, 1)] - (cz + sz)
    for axis in (2, 1, 0):
        e = along(e, axis, dual_back)
    solid = wall > 0.5
    return {n: jnp.where(solid, g[26 - n], g[n] - e[n]) for n in keep}


def row(ref, q, x):
    return ref[pl.ds(q * 32 + x, 8, stride=4), :]


def wall_row(ref, x):
    height = lax.broadcasted_iota(jnp.int32, (8, 128), 0)
    mask = ref[pl.ds(x, 8, stride=4), :]
    return jnp.where((height == 0) | (height == 7), 1, mask).astype(F32)


def merged(en, ey, xe, below):
    lane = lanes()
    low, high = lane % 8 < 3, lane % 8 >= 5

    def merge(own, lower, upper):
        own = own + jnp.where(high, rolly(upper, 4), 0.0)
        return own + jnp.where(low, rolly(lower, -4), 0.0) if below else own

    exl = [merge(en[0, k], en[1, k], en[2, k]) for k in range(3)]
    exr = [merge(en[3, k], en[4, k], en[5, k]) for k in range(3)]
    oxl = merge(ey[0, 0], xe[0, 0], xe[1, 0])
    oxr = merge(ey[0, 1], xe[0, 1], xe[1, 1])
    return exl, exr, oxl, oxr


def slot(q):
    return 3 * (q // 9) + q % 3


def pull_beside(packs, rates, gy):
    exl, exr, oxl, oxr = packs
    lane = lanes()
    left = lane < 8
    g = []
    for q, (cx, cy, cz) in enumerate(Q):
        s = slot(q)
        lo, hi = ((exl[2], oxr), (exl[1], exr[1]), (oxl, exr[2]))[cy + 1]
        v = jnp.where(left, rolly(lo, -8 * s - cx), rolly(hi, 8 - 8 * s - cx))
        g.append(rollz(v, -cz))
    m = []
    lo, hi = exl[1] + oxl, exr[1] + oxr
    for k in range(4):
        s = 9 + k
        m.append(jnp.where(left, rolly(lo, -8 * s), rolly(hi, 8 - 8 * s)))
    w = jnp.where(left, rolly(exl[1], -104), rolly(exr[1], -96))
    inv = 1.0 / jnp.where(m[0] > 0.0, m[0], 1.0)
    got = pull_back(g, [m[k] * inv for k in (1, 2, 3)], rates, w)
    for q, (cx, cy, cz) in enumerate(Q):
        if cy != 0:
            gy[q] = got[q]


def pull_row(x, packs, rates, cot, mb, xc, xm, gn):
    exl, exr = packs[0][0], packs[1][0]
    lane = lanes()
    first, last = lane == 0, lane == 127

    def source(q, x):
        if 0 <= x < ROWS:
            return row(cot, q, x)
        if x == -1:
            return xc[0, q]
        if x == -2:
            return xc[0, 18 + q]
        return xc[1, q - 9] if x == ROWS else xc[1, q]

    m = []
    for k in range(4):
        v = mb[x + 1, k]
        if x <= 0:
            v = v + xm[0, x + 1, k]
        if x >= 3:
            v = v + xm[1, x - 3, k]
        d = 8 * (9 + k) + x + 2
        v = v + jnp.where(first, rolly(exl, -d), 0.0)
        v = v + jnp.where(last, rolly(exr, 127 - d), 0.0)
        m.append(v)
    w = xm[0, 0, 4] if x < 0 else xm[1, 1, 4] if x == ROWS else mb[x + 1, 4]
    g = []
    for q, (cx, cy, cz) in enumerate(Q):
        v = source(q, x + cx)
        d = 8 * slot(q) + x + cx + 2
        if cy == 1:
            v = jnp.where(last, rolly(exr, 127 - d), rolly(v, -1))
        if cy == -1:
            v = jnp.where(first, rolly(exl, -d), rolly(v, 1))
        g.append(rollz(v, -cz))
    inv = 1.0 / m[0]
    keep = range(9) if x < 0 else range(18, 27) if x == ROWS else range(27)
    got = pull_back(g, [m[k] * inv for k in (1, 2, 3)], rates, w, keep)
    for q in keep:
        gn[q] = got[q]


def pull_first(x, rates, uck, mb, gn, gy, out):
    lane = lanes()
    first, last = lane == 0, lane == 127
    g = []
    for q, (cx, cy, cz) in enumerate(Q):
        v = gn(x + cx)[q]
        d = x + cx + 2
        if cy == 1:
            v = jnp.where(last, rolly(gy[q], 127 - 8 - d), rolly(v, -1))
        if cy == -1:
            v = jnp.where(first, rolly(gy[q], -d), rolly(v, 1))
        g.append(rollz(v, -cz))
    got = pull_back(g, [uck[x, k] for k in range(3)], rates, mb[x + 1, 4])
    for q in range(27):
        out[q] = got[q]


def exchange(
    sizes, ck_hbm, cot_hbm, wall_hbm, rates_hbm,
    cot, mb, ey, uck, rv, xc, xm, xe, en, upper, done,
    ck, wall, rates_ref, ehi, gy, load, ready, send, recv,
):
    nx, ny = sizes
    lane = lanes()

    def device(dx, dy):
        return (
            lax.rem(lax.axis_index("gx") + (dx + nx), nx),
            lax.rem(lax.axis_index("gy") + (dy + ny), ny),
        )

    def signal(sem, dx):
        for dy in (0, 1, -1):
            pl.semaphore_signal(sem, inc=1, device_id=device(dx, dy), device_id_type=MESH)

    barrier = pltpu.get_barrier_semaphore()
    signal(barrier, -1)
    loads = []
    for src, dst in ((cot_hbm.reshape(864, 128), cot), (ck_hbm, ck), (wall_hbm, wall), (rates_hbm, rates_ref)):
        loads.append(pltpu.make_async_copy(src, dst, load.at[len(loads)]))
        loads[-1].start()
    pl.semaphore_wait(barrier, 3)

    copies, late, soon = [], [], []

    def put(src, dst, dx, dy):
        n = len(copies)
        copies.append(
            pltpu.make_async_remote_copy(
                src_ref=src,
                dst_ref=dst,
                send_sem=send.at[n],
                recv_sem=recv.at[n],
                device_id=device(dx, dy),
                device_id_type=MESH,
            )
        )
        copies[-1].start()
        (late if dx == 1 else soon).append(copies[-1])

    put(cot_hbm.at[pl.ds(0, 18), :, 3], xc.at[0, pl.ds(0, 18)], 1, 0)
    put(cot_hbm.at[pl.ds(0, 9), :, 2], xc.at[0, pl.ds(18, 9)], 1, 0)
    signal(ready, 1)
    loads[0].wait()

    zero = jnp.zeros((8, 128), F32)
    first, last = lane == 0, lane == 127
    body = [[zero] * 4 for _ in range(6)]
    edge = [[zero] * 3 for _ in range(6)]
    acc = dict.fromkeys(("r0", "r1", "r2", "l0", "l1", "l2", "l0m"), zero)

    def add(name, v, d):
        acc[name] = jnp.where(lane == d, v, acc[name])

    def pack_cotangent(x):
        for i, (cx, cz) in enumerate([(a, c) for a in range(3) for c in range(3)]):
            d = 8 * i + x + 2
            v = rolly(row(cot, at(cx, 0, cz), x), d - 127)
            add("r0", v, d)
            add("r2", v, d - 1)
            v = rolly(row(cot, at(cx, 2, cz), x), d)
            add("l0", v, d)
            add("l2", v, d + 1)
            v = rolly(row(cot, at(cx, 1, cz), x), d - 127)
            add("r1", v, d)
            add("l1", v, d + 1)

    def pack_sums(r):
        outer = edge[r]
        outer = [outer[0], outer[1], jnp.where(first, outer[0], -outer[0]), outer[2]]
        for k in range(4):
            d = 8 * (9 + k) + r + 1
            v = rolly(body[r][k], d - 127)
            add("r1", v, d)
            add("l1", v, d + 1)
            v = rolly(outer[k], d)
            add("r0", v, d)
            add("l0m", v, d - 1)

    def pack_wall(x, w):
        d = 8 * 13 + x + 2
        v = rolly(w, d - 127)
        add("r1", v, d)
        add("l1", v, d + 1)

    def store_packs(ref):
        ref[0, 0] = acc["l0"] + rolly(acc["l0m"], 1)
        ref[1, 0] = rolly(acc["l1"], -1)
        ref[2, 0] = rolly(acc["l2"], -1)
        ref[0, 1] = acc["r0"]
        ref[1, 1] = acc["r1"]
        ref[2, 1] = rolly(acc["r2"], 1)

    def collide_row(x):
        w = wall_row(wall, x)
        mb[x + 1, 4] = w
        pack_wall(x, w)
        out, u = collide([row(ck, q, x) for q in range(27)], rates, w)
        for k in range(3):
            uck[x, k] = u[k]
        for a in range(3):
            sums, tilts = [], []
            for b in range(3):
                up = rollz(out[at(a, b, 2)], 1)
                down = rollz(out[at(a, b, 0)], -1)
                sums.append(out[at(a, b, 1)] + (up + down))
                tilts.append(up - down)
            ap, am = rolly(sums[2], 1), rolly(sums[0], -1)
            bp, bm = rolly(tilts[2], 1), rolly(tilts[0], -1)
            r = x + a
            outer = jnp.where(first, ap, am)
            edge[r][0] = edge[r][0] + outer
            edge[r][1] = edge[r][1] + (a - 1) * outer if a != 1 else edge[r][1]
            edge[r][2] = edge[r][2] + jnp.where(first, bp, bm)
            ap, am = jnp.where(first, 0.0, ap), jnp.where(last, 0.0, am)
            bp, bm = jnp.where(first, 0.0, bp), jnp.where(last, 0.0, bm)
            total = sums[1] + (ap + am)
            body[r][0] = body[r][0] + total
            if a != 1:
                body[r][1] = body[r][1] + (a - 1) * total
            body[r][2] = body[r][2] + (ap - am)
            body[r][3] = body[r][3] + (tilts[1] + (bp + bm))

    def store_sums(r):
        for k in range(4):
            mb[r, k] = body[r][k]
        pack_sums(r)

    pack_cotangent(3)
    pack_cotangent(2)
    for c in loads[1:]:
        c.wait()
    rates = halved_rates(rates_ref)
    mb[5, 4] = zero
    collide_row(3)
    collide_row(2)
    store_sums(5)
    store_sums(4)
    store_packs(ehi)
    put(ehi.at[:, 1], en.at[1], 1, 1)
    put(ehi.at[:, 0], en.at[4], 1, -1)
    put(mb.at[pl.ds(4, 2)], xm.at[0], 1, 0)
    put(ehi.at[0], xe.at[0], 1, 0)

    mb[0, 4] = zero
    pack_cotangent(1)
    pack_cotangent(0)
    collide_row(1)
    collide_row(0)
    for r in range(4):
        store_sums(r)
    store_packs(ey)
    pl.semaphore_wait(ready, 3)
    put(cot_hbm.at[pl.ds(9, 18), :, 0], xc.at[1, pl.ds(0, 18)], -1, 0)
    put(cot_hbm.at[pl.ds(18, 9), :, 1], xc.at[1, pl.ds(18, 9)], -1, 0)
    put(ey.at[:, 1], en.at[2], -1, 1)
    put(ey.at[:, 0], en.at[5], -1, -1)
    put(mb.at[pl.ds(0, 2)], xm.at[1], -1, 0)
    put(ey.at[0], xe.at[1], -1, 0)
    put(ey.at[:, 1], en.at[0], 0, 1)
    put(ey.at[:, 0], en.at[3], 0, -1)
    for n in range(27):
        rv[n] = jnp.full((8, 128), rates[n], F32)

    for c in soon:
        c.wait_recv()

    def known(n):
        return rv[n]

    packs = merged(en, ey, xe, False)
    for x in (4, 3, 2, 1):
        pull_row(x, packs, known, cot, mb, xc, xm, upper.at[x - 1])
    pull_beside(packs, known, gy)
    for x in (3, 2):
        pull_first(x, known, uck, mb, lambda x: upper.at[x - 1], gy, done.at[x - 2])
    for c in late:
        c.wait_recv()
    for c in copies:
        c.wait_send()


def finish(cot, mb, ey, uck, rv, xc, xm, xe, en, upper, done, out, lower, gy, ends, sems):
    def rates(n):
        return rv[n]

    def gn(x):
        return lower.at[x + 1] if x <= 0 else upper.at[x - 1]

    copies = []

    def put(src, x):
        copies.append(pltpu.make_async_copy(src, out.at[:, :, x], sems.at[x]))
        copies[-1].start()

    put(done.at[0], 2)
    put(done.at[1], 3)
    packs = merged(en, ey, xe, True)
    pull_beside(packs, rates, gy)
    pull_row(0, packs, rates, cot, mb, xc, xm, gn(0))
    pull_first(1, rates, uck, mb, gn, gy, ends.at[1])
    put(ends.at[1], 1)
    pull_row(-1, packs, rates, cot, mb, xc, xm, gn(-1))
    pull_first(0, rates, uck, mb, gn, gy, ends.at[0])
    put(ends.at[0], 0)
    for c in copies:
        c.wait()


def shards(sizes, checkpoint, rates, wall_mask, cotangent):
    ck = checkpoint.reshape(864, 128)
    wall, rates = wall_mask.reshape(32, 128), rates.reshape(1, 27)
    vmem, hbm = pl.BlockSpec(memory_space=pltpu.VMEM), pl.BlockSpec(memory_space=pltpu.HBM)
    small = dict(vmem_limit_bytes=16 << 20)

    def like(*shape):
        return jax.ShapeDtypeStruct(shape, F32)

    got = pl.pallas_call(
        functools.partial(exchange, sizes),
        out_shape=(
            like(864, 128), like(6, 5, 8, 128), like(3, 2, 8, 128), like(4, 3, 8, 128), like(27, 8, 128),
            like(2, 27, 8, 128), like(2, 2, 5, 8, 128), like(2, 2, 8, 128), like(6, 3, 8, 128),
            like(4, 27, 8, 128), like(2, 27, 8, 128),
        ),
        in_specs=[hbm] * 4,
        out_specs=(vmem,) * 11,
        scratch_shapes=[
            pltpu.VMEM((864, 128), F32),
            pltpu.VMEM((32, 128), jnp.int32),
            pltpu.SMEM((1, 27), F32),
            pltpu.VMEM((3, 2, 8, 128), F32),
            pltpu.VMEM((27, 8, 128), F32),
            pltpu.SemaphoreType.DMA((4,)),
            pltpu.SemaphoreType.REGULAR,
            pltpu.SemaphoreType.DMA((14,)),
            pltpu.SemaphoreType.DMA((14,)),
        ],
        compiler_params=pltpu.CompilerParams(collective_id=0, has_side_effects=True, **small),
        name="exchange",
    )(*[pltpu.with_memory_space_constraint(v, pltpu.HBM) for v in (ck, cotangent, wall, rates)])
    return pl.pallas_call(
        finish,
        out_shape=like(27, 8, 4, 128),
        in_specs=[vmem] * 11,
        out_specs=hbm,
        scratch_shapes=[
            pltpu.VMEM((2, 27, 8, 128), F32),
            pltpu.VMEM((27, 8, 128), F32),
            pltpu.VMEM((2, 27, 8, 128), F32),
            pltpu.SemaphoreType.DMA((4,)),
        ],
        compiler_params=pltpu.CompilerParams(**small),
        name="finish",
    )(*got)


def solution(mesh):
    sizes = (mesh.shape["gx"], mesh.shape["gy"])
    in_specs = (P(None, None, "gx", "gy"), P(), P(None, "gx", "gy"), P(None, None, "gx", "gy"))
    out_specs = P(None, None, "gx", "gy")
    return jax.shard_map(
        functools.partial(shards, sizes), mesh=mesh, in_specs=in_specs, out_specs=out_specs, check_vma=False
    )
```

```python
import functools

import jax
import jax.numpy as jnp
from jax import lax
from jax.experimental import pallas as pl
from jax.experimental.pallas import tpu as pltpu
from jax.sharding import PartitionSpec as P

F32 = jnp.float32
MESH = pl.DeviceIdType.MESH
ROWS = 4
Q = [(a, b, c) for a in (-1, 0, 1) for b in (-1, 0, 1) for c in (-1, 0, 1)]
THIRD = 1.0 / 3.0
NINTH = 1.0 / 9.0


def rollz(v, s):
    return v if s == 0 else pltpu.roll(v, s % 8, 0)


def rolly(v, s):
    return v if s % 128 == 0 else pltpu.roll(v, s % 128, 1)


def lanes():
    return lax.broadcasted_iota(jnp.int32, (8, 128), 1)


def along(values, axis, fn):
    out = [None] * 27
    step = (9, 3, 1)[axis]
    for i in range(27):
        if (i // step) % 3 == 0:
            out[i], out[i + step], out[i + 2 * step] = fn(
                values[i], values[i + step], values[i + 2 * step]
            )
    return out


def to_moments(a, b, c):
    s = a + c
    return s + b, c - a, s


def from_halved(m0, m1, m2):
    a, c = m2 - m1, m2 + m1
    return a, m0 - (a + c), c


def dual_doubled(a, b, c):
    return b, c - a, (a + c) - (b + b)


def dual_back(m0, m1, m2):
    s = m0 + m2
    return s - m1, m0, s + m1


def at(i, j, k):
    return 9 * i + 3 * j + k


def halved_rates(rates_ref):
    return [
        rates_ref[0, n] * (0.5 ** sum(p > 0 for p in (n // 9, n // 3 % 3, n % 3)))
        for n in range(27)
    ]


def collide(f, rates, wall):
    m = f
    for axis in (2, 1, 0):
        m = along(m, axis, to_moments)
    rho, jx, jy, jz = m[0], m[9], m[3], m[1]
    inv = 1.0 / rho
    ux, uy, uz = jx * inv, jy * inv, jz * inv
    xx, yy, zz = jx * ux, jy * uy, jz * uz
    xy, xz, yz = jx * uy, jx * uz, jy * uz
    r3, r9 = rho * THIRD, rho * NINTH
    x3, y3, z3 = jx * THIRD, jy * THIRD, jz * THIRD
    eq = [None] * 27
    eq[at(0, 0, 0)] = rho
    eq[at(1, 0, 0)], eq[at(0, 1, 0)], eq[at(0, 0, 1)] = jx, jy, jz
    eq[at(2, 0, 0)], eq[at(0, 2, 0)], eq[at(0, 0, 2)] = r3 + xx, r3 + yy, r3 + zz
    eq[at(1, 1, 0)], eq[at(1, 0, 1)], eq[at(0, 1, 1)] = xy, xz, yz
    eq[at(1, 2, 0)] = eq[at(1, 0, 2)] = x3
    eq[at(2, 1, 0)] = eq[at(0, 1, 2)] = y3
    eq[at(2, 0, 1)] = eq[at(0, 2, 1)] = z3
    eq[at(1, 2, 2)], eq[at(2, 1, 2)], eq[at(2, 2, 1)] = x3 * THIRD, y3 * THIRD, z3 * THIRD
    eq[at(1, 1, 2)], eq[at(1, 2, 1)], eq[at(2, 1, 1)] = xy * THIRD, xz * THIRD, yz * THIRD
    eq[at(2, 2, 0)] = r9 + (xx + yy) * THIRD
    eq[at(2, 0, 2)] = r9 + (xx + zz) * THIRD
    eq[at(0, 2, 2)] = r9 + (yy + zz) * THIRD
    eq[at(2, 2, 2)] = r9 * THIRD + (xx + yy + zz) * NINTH
    d = [
        m[n] * rates[n] if eq[n] is None else (m[n] - eq[n]) * rates[n]
        for n in range(27)
    ]
    for axis in (0, 1, 2):
        d = along(d, axis, from_halved)
    solid = wall > 0.5
    out = [jnp.where(solid, f[26 - n], f[n] - d[n]) for n in range(27)]
    return out, (ux, uy, uz)


def pull_back(g, u, rates, wall, keep=range(27)):
    ux, uy, uz = u
    e = g
    for axis in (2, 1, 0):
        e = along(e, axis, dual_doubled)
    e = [e[n] * rates(n) for n in range(27)]
    e222 = e[at(2, 2, 2)] * NINTH
    pair_xy, pair_xz, pair_yz = e[at(2, 2, 0)], e[at(2, 0, 2)], e[at(0, 2, 2)]
    pxx = e[at(2, 0, 0)] + (pair_xy + pair_xz) * THIRD + e222
    pyy = e[at(0, 2, 0)] + (pair_xy + pair_yz) * THIRD + e222
    pzz = e[at(0, 0, 2)] + (pair_xz + pair_yz) * THIRD + e222
    pxy = e[at(1, 1, 0)] + e[at(1, 1, 2)] * THIRD
    pxz = e[at(1, 0, 1)] + e[at(1, 2, 1)] * THIRD
    pyz = e[at(0, 1, 1)] + e[at(2, 1, 1)] * THIRD
    rho = (
        e[0]
        + (e[at(2, 0, 0)] + e[at(0, 2, 0)] + e[at(0, 0, 2)] + e222) * THIRD
        + (pair_xy + pair_xz + pair_yz) * NINTH
    )
    cx = e[at(1, 0, 0)] + (e[at(1, 2, 0)] + e[at(1, 0, 2)]) * THIRD + e[at(1, 2, 2)] * NINTH
    cy = e[at(0, 1, 0)] + (e[at(2, 1, 0)] + e[at(0, 1, 2)]) * THIRD + e[at(2, 1, 2)] * NINTH
    cz = e[at(0, 0, 1)] + (e[at(2, 0, 1)] + e[at(0, 2, 1)]) * THIRD + e[at(2, 2, 1)] * NINTH
    sx = (pxx + pxx) * ux + pxy * uy + pxz * uz
    sy = (pyy + pyy) * uy + pxy * ux + pyz * uz
    sz = (pzz + pzz) * uz + pxz * ux + pyz * uy
    rho = rho - 0.5 * (ux * sx + uy * sy + uz * sz)
    e[at(0, 0, 0)] = e[at(0, 0, 0)] - rho
    e[at(1, 0, 0)] = e[at(1, 0, 0)] - (cx + sx)
    e[at(0, 1, 0)] = e[at(0, 1, 0)] - (cy + sy)
    e[at(0, 0, 1)] = e[at(0, 0, 1)] - (cz + sz)
    for axis in (2, 1, 0):
        e = along(e, axis, dual_back)
    solid = wall > 0.5
    return {n: jnp.where(solid, g[26 - n], g[n] - e[n]) for n in keep}


def row(ref, q, x):
    return ref[pl.ds(q * 32 + x, 8, stride=4), :]


def wall_row(ref, x):
    height = lax.broadcasted_iota(jnp.int32, (8, 128), 0)
    mask = ref[pl.ds(x, 8, stride=4), :]
    return jnp.where((height == 0) | (height == 7), 1, mask).astype(F32)


def merged(en, ep, ey, below):
    lane = lanes() % 8

    def ends(v, k, low):
        if low:
            return jnp.where(lane < (2 if k == 2 else 3), rolly(v, (-4, -1, -7)[k]), 0.0)
        return jnp.where(lane >= (6 if k == 2 else 5), rolly(v, (4, 1, -1)[k]), 0.0)

    def merge(own, k, which):
        own = own + ends(ep[3 + which], k, False)
        return own + ends(ep[which], k, True) if below else own

    exl = [merge(en[0, k], k, 0) for k in range(3)]
    exr = [merge(en[1, k], k, 1) for k in range(3)]
    oxl = merge(ey[0, 0], 0, 2)
    oxr = merge(ey[0, 1], 1, 2)
    return exl, exr, oxl, oxr


def field(r, k):
    if r == 0:
        return {0: 2, 2: 3, 3: 4, 1: 0, 4: 1}[k]
    return 5 * r + {0: 0, 2: 1, 3: 2, 1: 3, 4: 4}[k]


def slot(q):
    return 3 * (q // 9) + q % 3


def pull_beside(packs, rates, gy):
    exl, exr, oxl, oxr = packs
    lane = lanes()
    left = lane < 8
    g = []
    for q, (cx, cy, cz) in enumerate(Q):
        s = slot(q)
        lo, hi = ((exl[2], oxr), (exl[1], exr[1]), (oxl, exr[2]))[cy + 1]
        v = jnp.where(left, rolly(lo, -8 * s - cx), rolly(hi, 8 - 8 * s - cx))
        g.append(rollz(v, -cz))
    m = []
    lo, hi = exl[1] + oxl, exr[1] + oxr
    for k in range(4):
        s = 9 + k
        m.append(jnp.where(left, rolly(lo, -8 * s), rolly(hi, 8 - 8 * s)))
    w = jnp.where(left, rolly(exl[1], -104), rolly(exr[1], -96))
    inv = 1.0 / jnp.where(m[0] > 0.0, m[0], 1.0)
    got = pull_back(g, [m[k] * inv for k in (1, 2, 3)], rates, w)
    for q, (cx, cy, cz) in enumerate(Q):
        if cy != 0:
            gy[q] = got[q]


def pull_row(x, exl, exr, rates, cot, mb, xc, xm, gn):
    lane = lanes()
    first, last = lane == 0, lane == 127

    def source(q, x):
        if 0 <= x < ROWS:
            return row(cot, q, x)
        if x == -1:
            return xc[0, q]
        if x == -2:
            return xc[0, 18 + q]
        return xc[1, q - 9] if x == ROWS else xc[1, q]

    m = []
    for k in range(4):
        v = mb[field(x + 1, k)]
        if x == -1:
            v = v + xm[0, field(1, k) - 5]
        if x == 0:
            v = v + xm[0, field(1, 0 if k == 1 else k)]
        if x == 3:
            v = v - xm[1, 0] if k == 1 else v + xm[1, field(0, k) - 2]
        if x == 4:
            v = v + xm[1, field(1, k) - 2]
        d = 8 * (9 + k) + x + 2
        v = v + jnp.where(first, rolly(exl, -d), 0.0)
        v = v + jnp.where(last, rolly(exr, 127 - d), 0.0)
        m.append(v)
    w = xm[0, 4] if x < 0 else xm[1, 7] if x == ROWS else mb[field(x + 1, 4)]
    g = []
    for q, (cx, cy, cz) in enumerate(Q):
        v = source(q, x + cx)
        d = 8 * slot(q) + x + cx + 2
        if cy == 1:
            v = jnp.where(last, rolly(exr, 127 - d), rolly(v, -1))
        if cy == -1:
            v = jnp.where(first, rolly(exl, -d), rolly(v, 1))
        g.append(rollz(v, -cz))
    inv = 1.0 / m[0]
    keep = range(9) if x < 0 else range(18, 27) if x == ROWS else range(27)
    got = pull_back(g, [m[k] * inv for k in (1, 2, 3)], rates, w, keep)
    for q in keep:
        gn[q] = got[q]


def pull_first(x, rates, uck, mb, gn, gy, out):
    lane = lanes()
    first, last = lane == 0, lane == 127
    g = []
    for q, (cx, cy, cz) in enumerate(Q):
        v = gn(x + cx)[q]
        d = x + cx + 2
        if cy == 1:
            v = jnp.where(last, rolly(gy[q], 127 - 8 - d), rolly(v, -1))
        if cy == -1:
            v = jnp.where(first, rolly(gy[q], -d), rolly(v, 1))
        g.append(rollz(v, -cz))
    got = pull_back(g, [uck[x, k] for k in range(3)], rates, mb[field(x + 1, 4)])
    for q in range(27):
        out[q] = got[q]


def exchange(
    sizes, ck_hbm, cot_hbm, wall_hbm, rates_hbm,
    cot, mb, uck, rv, xc, xm, upper, gy, done, beside,
    ck, wall, rates_ref, ey, eh, el, en, ep, load, ready, send, recv,
):
    nx, ny = sizes
    lane = lanes()

    def device(dx, dy):
        return (
            lax.rem(lax.axis_index("gx") + (dx + nx), nx),
            lax.rem(lax.axis_index("gy") + (dy + ny), ny),
        )

    def signal(sem, dx):
        for dy in (0, 1, -1):
            pl.semaphore_signal(sem, inc=1, device_id=device(dx, dy), device_id_type=MESH)

    place = lax.rem(lax.axis_index("gx"), nx // 2)
    opens, closes = place == 0, place == nx // 2 - 1
    barrier = pltpu.get_barrier_semaphore()
    signal(barrier, -1)

    @pl.when(jnp.logical_not(closes))
    def _():
        for dy in (1, -1):
            pl.semaphore_signal(barrier, inc=1, device_id=device(0, dy), device_id_type=MESH)

    loads = []
    for src, dst in ((cot_hbm.reshape(864, 128), cot), (ck_hbm, ck), (wall_hbm, wall), (rates_hbm, rates_ref)):
        loads.append(pltpu.make_async_copy(src, dst, load.at[len(loads)]))
        loads[-1].start()

    @pl.when(closes)
    def _():
        pl.semaphore_wait(barrier, 3)

    @pl.when(jnp.logical_not(closes))
    def _():
        pl.semaphore_wait(barrier, 5)


    copies, late, soon = [], [], []

    def copy_to(src, dst, dx, dy):
        n = len(copies)
        copies.append(
            pltpu.make_async_remote_copy(
                src_ref=src,
                dst_ref=dst,
                send_sem=send.at[n],
                recv_sem=recv.at[n],
                device_id=device(dx, dy),
                device_id_type=MESH,
            )
        )
        (late if dx == 1 else soon).append(copies[-1])
        return copies[-1]

    def put(src, dst, dx, dy):
        copy_to(src, dst, dx, dy).start()

    put(cot_hbm.at[pl.ds(0, 18), :, 3], xc.at[0, pl.ds(0, 18)], 1, 0)
    signal(ready, 1)
    loads[0].wait()

    zero = jnp.zeros((8, 128), F32)
    first, last = lane == 0, lane == 127
    body = [[zero] * 4 for _ in range(6)]
    edge = [[zero] * 3 for _ in range(6)]
    acc = dict.fromkeys(("r0", "r1", "r2", "l0", "l1", "l2", "l0m"), zero)

    def add(name, v, d):
        acc[name] = jnp.where(lane == d, v, acc[name])

    def pack_cotangent(x):
        for i, (cx, cz) in enumerate([(a, c) for a in range(3) for c in range(3)]):
            d = 8 * i + x + 2
            v = rolly(row(cot, at(cx, 0, cz), x), d - 127)
            add("r0", v, d)
            add("r2", v, d - 1)
            v = rolly(row(cot, at(cx, 2, cz), x), d)
            add("l0", v, d)
            add("l2", v, d + 1)
            v = rolly(row(cot, at(cx, 1, cz), x), d - 127)
            add("r1", v, d)
            add("l1", v, d + 1)

    def pack_sums(r):
        outer = edge[r]
        outer = [outer[0], outer[1], jnp.where(first, outer[0], -outer[0]), outer[2]]
        for k in range(4):
            d = 8 * (9 + k) + r + 1
            v = rolly(body[r][k], d - 127)
            add("r1", v, d)
            add("l1", v, d + 1)
            v = rolly(outer[k], d)
            add("r0", v, d)
            add("l0m", v, d - 1)

    def pack_wall(x, w):
        d = 8 * 13 + x + 2
        v = rolly(w, d - 127)
        add("r1", v, d)
        add("l1", v, d + 1)

    def packed():
        left = acc["l0"] + rolly(acc["l0m"], 1), rolly(acc["l1"], -1), rolly(acc["l2"], -1)
        right = acc["r0"], acc["r1"], rolly(acc["r2"], 1)
        return left, right

    def collide_row(x):
        w = wall_row(wall, x)
        mb[field(x + 1, 4)] = w
        pack_wall(x, w)
        out, u = collide([row(ck, q, x) for q in range(27)], rates, w)
        for k in range(3):
            uck[x, k] = u[k]
        for a in range(3):
            sums, tilts = [], []
            for b in range(3):
                up = rollz(out[at(a, b, 2)], 1)
                down = rollz(out[at(a, b, 0)], -1)
                sums.append(out[at(a, b, 1)] + (up + down))
                tilts.append(up - down)
            ap, am = rolly(sums[2], 1), rolly(sums[0], -1)
            bp, bm = rolly(tilts[2], 1), rolly(tilts[0], -1)
            r = x + a
            outer = jnp.where(first, ap, am)
            edge[r][0] = edge[r][0] + outer
            edge[r][1] = edge[r][1] + (a - 1) * outer if a != 1 else edge[r][1]
            edge[r][2] = edge[r][2] + jnp.where(first, bp, bm)
            ap, am = jnp.where(first, 0.0, ap), jnp.where(last, 0.0, am)
            bp, bm = jnp.where(first, 0.0, bp), jnp.where(last, 0.0, bm)
            total = sums[1] + (ap + am)
            body[r][0] = body[r][0] + total
            if a != 1:
                body[r][1] = body[r][1] + (a - 1) * total
            body[r][2] = body[r][2] + (ap - am)
            body[r][3] = body[r][3] + (tilts[1] + (bp + bm))

    def store_sums(r):
        for k in range(4):
            mb[field(r, k)] = body[r][k]
        pack_sums(r)

    pack_cotangent(3)
    pack_cotangent(2)
    for c in loads[1:]:
        c.wait()
    rates = halved_rates(rates_ref)
    collide_row(3)
    collide_row(2)
    store_sums(5)
    store_sums(4)
    left, right = packed()
    eh[0] = right[0] + (rolly(right[1], -3) + rolly(right[2], 3))
    eh[1] = left[0] + (rolly(left[1], -3) + rolly(left[2], 3))
    eh[2] = left[0] + rolly(right[0], -3)
    put(eh.at[0], ep.at[0], 1, 1)
    put(eh.at[1], ep.at[1], 1, -1)
    put(eh.at[2], ep.at[2], 1, 0)
    put(mb.at[pl.ds(20, 8)], xm.at[0], 1, 0)
    put(cot_hbm.at[pl.ds(0, 9), :, 2], xc.at[0, pl.ds(18, 9)], 1, 0)

    pack_cotangent(1)
    pack_cotangent(0)
    collide_row(1)
    collide_row(0)
    for r in range(4):
        store_sums(r)
    left, right = packed()
    for k in range(3):
        ey[k, 0] = left[k]
        ey[k, 1] = right[k]
    rest = (lane % 8 > 0) & (lane % 8 < 4)
    left = [jnp.where(rest, v, 0.0) for v in left]
    right = [jnp.where(rest, v, 0.0) for v in right]
    el[0] = right[0] + (rolly(right[1], 3) + rolly(right[2], 5))
    el[1] = left[0] + (rolly(left[1], 3) + rolly(left[2], 5))
    el[2] = left[0] + rolly(right[0], 3)

    @pl.when(closes)
    def _():
        pl.semaphore_wait(ready, 3)

    put(ey.at[:, 1], en.at[0], 0, 1)
    put(ey.at[:, 0], en.at[1], 0, -1)
    back = [
        copy_to(cot_hbm.at[pl.ds(9, 18), :, 0], xc.at[1, pl.ds(0, 18)], -1, 0),
        copy_to(el.at[0], ep.at[3], -1, 1),
        copy_to(el.at[1], ep.at[4], -1, -1),
        copy_to(el.at[2], ep.at[5], -1, 0),
        copy_to(mb.at[pl.ds(2, 8)], xm.at[1], -1, 0),
        copy_to(cot_hbm.at[pl.ds(18, 9), :, 1], xc.at[1, pl.ds(18, 9)], -1, 0),
    ]

    @pl.when(jnp.logical_not(opens | closes))
    def _():
        pl.semaphore_wait(ready, 3)

    @pl.when(jnp.logical_not(opens))
    def _():
        for c in back:
            c.start()

    for n in range(27):
        rv[n] = jnp.full((8, 128), rates[n], F32)

    for c in soon:
        c.wait_recv()

    def known(n):
        return rv[n]

    def gn(x):
        return upper.at[x]

    packs = merged(en, ep, ey, False)
    exl, exr = packs[0][0], packs[1][0]
    for x in (4, 3, 2, 1):
        pull_row(x, exl, exr, known, cot, mb, xc, xm, gn(x))
    pull_beside(packs, known, gy)
    for x in (3, 2):
        pull_first(x, known, uck, mb, gn, gy, done.at[x - 1])

    @pl.when(opens)
    def _():
        pl.semaphore_wait(ready, 3)
        for c in back:
            c.start()

    for c in late[:-1]:
        c.wait_recv()
    packs = merged(en, ep, ey, True)
    exl, exr = packs[0][0], packs[1][0]
    beside[0], beside[1] = exl, exr
    pull_row(0, exl, exr, known, cot, mb, xc, xm, gn(0))
    pull_beside(packs, known, gy)
    pull_first(1, known, uck, mb, gn, gy, done.at[0])
    late[-1].wait_recv()
    for c in copies:
        c.wait_send()


def finish(cot, mb, uck, rv, xc, xm, upper, gy, done, beside, out, lower, end, sems):
    def rates(n):
        return rv[n]

    def gn(x):
        return lower if x < 0 else upper.at[x]

    copies = []

    def put(src, x):
        copies.append(pltpu.make_async_copy(src, out.at[:, :, x], sems.at[x]))
        copies[-1].start()

    for x in (1, 2, 3):
        put(done.at[x - 1], x)
    pull_row(-1, beside[0], beside[1], rates, cot, mb, xc, xm, lower)
    pull_first(0, rates, uck, mb, gn, gy, end)
    put(end, 0)
    for c in copies:
        c.wait()


def shards(sizes, checkpoint, rates, wall_mask, cotangent):
    ck = checkpoint.reshape(864, 128)
    wall, rates = wall_mask.reshape(32, 128), rates.reshape(1, 27)
    vmem, hbm = pl.BlockSpec(memory_space=pltpu.VMEM), pl.BlockSpec(memory_space=pltpu.HBM)
    small = dict(vmem_limit_bytes=16 << 20)

    def like(*shape):
        return jax.ShapeDtypeStruct(shape, F32)

    got = pl.pallas_call(
        functools.partial(exchange, sizes),
        out_shape=(
            like(864, 128), like(30, 8, 128), like(4, 3, 8, 128), like(27, 8, 128), like(2, 27, 8, 128),
            like(2, 8, 8, 128), like(5, 27, 8, 128), like(27, 8, 128), like(3, 27, 8, 128), like(2, 8, 128),
        ),
        in_specs=[hbm] * 4,
        out_specs=(vmem,) * 10,
        scratch_shapes=[
            pltpu.VMEM((864, 128), F32),
            pltpu.VMEM((32, 128), jnp.int32),
            pltpu.SMEM((1, 27), F32),
            pltpu.VMEM((3, 2, 8, 128), F32),
            pltpu.VMEM((3, 8, 128), F32),
            pltpu.VMEM((3, 8, 128), F32),
            pltpu.VMEM((2, 3, 8, 128), F32),
            pltpu.VMEM((6, 8, 128), F32),
            pltpu.SemaphoreType.DMA((4,)),
            pltpu.SemaphoreType.REGULAR,
            pltpu.SemaphoreType.DMA((14,)),
            pltpu.SemaphoreType.DMA((14,)),
        ],
        compiler_params=pltpu.CompilerParams(collective_id=0, has_side_effects=True, **small),
        name="exchange",
    )(*[pltpu.with_memory_space_constraint(v, pltpu.HBM) for v in (ck, cotangent, wall, rates)])
    return pl.pallas_call(
        finish,
        out_shape=like(27, 8, 4, 128),
        in_specs=[vmem] * 10,
        out_specs=hbm,
        scratch_shapes=[
            pltpu.VMEM((27, 8, 128), F32),
            pltpu.VMEM((27, 8, 128), F32),
            pltpu.SemaphoreType.DMA((4,)),
        ],
        compiler_params=pltpu.CompilerParams(**small),
        name="finish",
    )(*got)


def solution(mesh):
    sizes = (mesh.shape["gx"], mesh.shape["gy"])
    in_specs = (P(None, None, "gx", "gy"), P(), P(None, "gx", "gy"), P(None, None, "gx", "gy"))
    out_specs = P(None, None, "gx", "gy")
    return jax.shard_map(
        functools.partial(shards, sizes), mesh=mesh, in_specs=in_specs, out_specs=out_specs, check_vma=False
    )
```

```python
import functools

import jax
import jax.numpy as jnp
from jax import lax
from jax.experimental import pallas as pl
from jax.experimental.pallas import tpu as pltpu
from jax.sharding import PartitionSpec as P

F32 = jnp.float32
MESH = pl.DeviceIdType.MESH
ROWS = 4
Q = [(a, b, c) for a in (-1, 0, 1) for b in (-1, 0, 1) for c in (-1, 0, 1)]
THIRD = 1.0 / 3.0
NINTH = 1.0 / 9.0


def rollz(v, s):
    return v if s == 0 else pltpu.roll(v, s % 8, 0)


def rolly(v, s):
    return v if s % 128 == 0 else pltpu.roll(v, s % 128, 1)


def lanes():
    return lax.broadcasted_iota(jnp.int32, (8, 128), 1)


def along(values, axis, fn):
    out = [None] * 27
    step = (9, 3, 1)[axis]
    for i in range(27):
        if (i // step) % 3 == 0:
            out[i], out[i + step], out[i + 2 * step] = fn(
                values[i], values[i + step], values[i + 2 * step]
            )
    return out


def to_moments(a, b, c):
    s = a + c
    return s + b, c - a, s


def from_halved(m0, m1, m2):
    a, c = m2 - m1, m2 + m1
    return a, m0 - (a + c), c


def dual_doubled(a, b, c):
    return b, c - a, (a + c) - (b + b)


def dual_back(m0, m1, m2):
    s = m0 + m2
    return s - m1, m0, s + m1


def at(i, j, k):
    return 9 * i + 3 * j + k


def halved_rates(rates_ref):
    return [
        rates_ref[0, n] * (0.5 ** sum(p > 0 for p in (n // 9, n // 3 % 3, n % 3)))
        for n in range(27)
    ]


def collide(f, rates, wall):
    m = f
    for axis in (2, 1, 0):
        m = along(m, axis, to_moments)
    rho, jx, jy, jz = m[0], m[9], m[3], m[1]
    inv = 1.0 / rho
    ux, uy, uz = jx * inv, jy * inv, jz * inv
    xx, yy, zz = jx * ux, jy * uy, jz * uz
    xy, xz, yz = jx * uy, jx * uz, jy * uz
    r3, r9 = rho * THIRD, rho * NINTH
    x3, y3, z3 = jx * THIRD, jy * THIRD, jz * THIRD
    eq = [None] * 27
    eq[at(0, 0, 0)] = rho
    eq[at(1, 0, 0)], eq[at(0, 1, 0)], eq[at(0, 0, 1)] = jx, jy, jz
    eq[at(2, 0, 0)], eq[at(0, 2, 0)], eq[at(0, 0, 2)] = r3 + xx, r3 + yy, r3 + zz
    eq[at(1, 1, 0)], eq[at(1, 0, 1)], eq[at(0, 1, 1)] = xy, xz, yz
    eq[at(1, 2, 0)] = eq[at(1, 0, 2)] = x3
    eq[at(2, 1, 0)] = eq[at(0, 1, 2)] = y3
    eq[at(2, 0, 1)] = eq[at(0, 2, 1)] = z3
    eq[at(1, 2, 2)], eq[at(2, 1, 2)], eq[at(2, 2, 1)] = x3 * THIRD, y3 * THIRD, z3 * THIRD
    eq[at(1, 1, 2)], eq[at(1, 2, 1)], eq[at(2, 1, 1)] = xy * THIRD, xz * THIRD, yz * THIRD
    eq[at(2, 2, 0)] = r9 + (xx + yy) * THIRD
    eq[at(2, 0, 2)] = r9 + (xx + zz) * THIRD
    eq[at(0, 2, 2)] = r9 + (yy + zz) * THIRD
    eq[at(2, 2, 2)] = r9 * THIRD + (xx + yy + zz) * NINTH
    d = [
        m[n] * rates[n] if eq[n] is None else (m[n] - eq[n]) * rates[n]
        for n in range(27)
    ]
    for axis in (0, 1, 2):
        d = along(d, axis, from_halved)
    solid = wall > 0.5
    out = [jnp.where(solid, f[26 - n], f[n] - d[n]) for n in range(27)]
    return out, (ux, uy, uz)


def pull_back(g, u, rates, wall, keep=range(27)):
    ux, uy, uz = u
    e = g
    for axis in (2, 1, 0):
        e = along(e, axis, dual_doubled)
    e = [e[n] * rates(n) for n in range(27)]
    e222 = e[at(2, 2, 2)] * NINTH
    pair_xy, pair_xz, pair_yz = e[at(2, 2, 0)], e[at(2, 0, 2)], e[at(0, 2, 2)]
    pxx = e[at(2, 0, 0)] + (pair_xy + pair_xz) * THIRD + e222
    pyy = e[at(0, 2, 0)] + (pair_xy + pair_yz) * THIRD + e222
    pzz = e[at(0, 0, 2)] + (pair_xz + pair_yz) * THIRD + e222
    pxy = e[at(1, 1, 0)] + e[at(1, 1, 2)] * THIRD
    pxz = e[at(1, 0, 1)] + e[at(1, 2, 1)] * THIRD
    pyz = e[at(0, 1, 1)] + e[at(2, 1, 1)] * THIRD
    rho = (
        e[0]
        + (e[at(2, 0, 0)] + e[at(0, 2, 0)] + e[at(0, 0, 2)] + e222) * THIRD
        + (pair_xy + pair_xz + pair_yz) * NINTH
    )
    cx = e[at(1, 0, 0)] + (e[at(1, 2, 0)] + e[at(1, 0, 2)]) * THIRD + e[at(1, 2, 2)] * NINTH
    cy = e[at(0, 1, 0)] + (e[at(2, 1, 0)] + e[at(0, 1, 2)]) * THIRD + e[at(2, 1, 2)] * NINTH
    cz = e[at(0, 0, 1)] + (e[at(2, 0, 1)] + e[at(0, 2, 1)]) * THIRD + e[at(2, 2, 1)] * NINTH
    sx = (pxx + pxx) * ux + pxy * uy + pxz * uz
    sy = (pyy + pyy) * uy + pxy * ux + pyz * uz
    sz = (pzz + pzz) * uz + pxz * ux + pyz * uy
    rho = rho - 0.5 * (ux * sx + uy * sy + uz * sz)
    e[at(0, 0, 0)] = e[at(0, 0, 0)] - rho
    e[at(1, 0, 0)] = e[at(1, 0, 0)] - (cx + sx)
    e[at(0, 1, 0)] = e[at(0, 1, 0)] - (cy + sy)
    e[at(0, 0, 1)] = e[at(0, 0, 1)] - (cz + sz)
    for axis in (2, 1, 0):
        e = along(e, axis, dual_back)
    solid = wall > 0.5
    return {n: jnp.where(solid, g[26 - n], g[n] - e[n]) for n in keep}


def row(ref, q, x):
    return ref[pl.ds(q * 32 + x, 8, stride=4), :]


def wall_row(ref, x):
    height = lax.broadcasted_iota(jnp.int32, (8, 128), 0)
    mask = ref[pl.ds(x, 8, stride=4), :]
    return jnp.where((height == 0) | (height == 7), 1, mask).astype(F32)


def merged(en, ep, ey, below):
    lane = lanes() % 8

    def ends(v, k, low):
        if low:
            return jnp.where(lane < (2 if k == 2 else 3), rolly(v, (-4, -1, -7)[k]), 0.0)
        return jnp.where(lane >= (6 if k == 2 else 5), rolly(v, (4, 1, -1)[k]), 0.0)

    def merge(own, k, which):
        own = own + ends(ep[3 + which], k, False)
        return own + ends(ep[which], k, True) if below else own

    exl = [merge(en[0, k], k, 0) for k in range(3)]
    exr = [merge(en[1, k], k, 1) for k in range(3)]
    oxl = merge(ey[0, 0], 0, 2)
    oxr = merge(ey[0, 1], 1, 2)
    return exl, exr, oxl, oxr


def field(r, k):
    if r == 0:
        return {0: 2, 2: 3, 3: 4, 1: 0, 4: 1}[k]
    return 5 * r + {0: 0, 2: 1, 3: 2, 1: 3, 4: 4}[k]


def slot(q):
    return 3 * (q // 9) + q % 3


def pull_beside(packs, rates, gy):
    exl, exr, oxl, oxr = packs
    lane = lanes()
    left = lane < 8
    g = []
    for q, (cx, cy, cz) in enumerate(Q):
        s = slot(q)
        lo, hi = ((exl[2], oxr), (exl[1], exr[1]), (oxl, exr[2]))[cy + 1]
        v = jnp.where(left, rolly(lo, -8 * s - cx), rolly(hi, 8 - 8 * s - cx))
        g.append(rollz(v, -cz))
    m = []
    lo, hi = exl[1] + oxl, exr[1] + oxr
    for k in range(4):
        s = 9 + k
        m.append(jnp.where(left, rolly(lo, -8 * s), rolly(hi, 8 - 8 * s)))
    w = jnp.where(left, rolly(exl[1], -104), rolly(exr[1], -96))
    inv = 1.0 / jnp.where(m[0] > 0.0, m[0], 1.0)
    got = pull_back(g, [m[k] * inv for k in (1, 2, 3)], rates, w)
    for q, (cx, cy, cz) in enumerate(Q):
        if cy != 0:
            gy[q] = got[q]


def pull_row(x, exl, exr, rates, cot, mb, xc, xm, gn):
    lane = lanes()
    first, last = lane == 0, lane == 127

    def source(q, x):
        if 0 <= x < ROWS:
            return row(cot, q, x)
        if x == -1:
            return xc[0, q]
        if x == -2:
            return xc[0, 18 + q]
        return xc[1, q - 9] if x == ROWS else xc[1, q]

    m = []
    for k in range(4):
        v = mb[field(x + 1, k)]
        if x == -1:
            v = v + xm[0, field(1, k) - 5]
        if x == 0:
            v = v + xm[0, field(1, 0 if k == 1 else k)]
        if x == 3:
            v = v - xm[1, 0] if k == 1 else v + xm[1, field(0, k) - 2]
        if x == 4:
            v = v + xm[1, field(1, k) - 2]
        d = 8 * (9 + k) + x + 2
        v = v + jnp.where(first, rolly(exl, -d), 0.0)
        v = v + jnp.where(last, rolly(exr, 127 - d), 0.0)
        m.append(v)
    w = xm[0, 4] if x < 0 else xm[1, 7] if x == ROWS else mb[field(x + 1, 4)]
    g = []
    for q, (cx, cy, cz) in enumerate(Q):
        v = source(q, x + cx)
        d = 8 * slot(q) + x + cx + 2
        if cy == 1:
            v = jnp.where(last, rolly(exr, 127 - d), rolly(v, -1))
        if cy == -1:
            v = jnp.where(first, rolly(exl, -d), rolly(v, 1))
        g.append(rollz(v, -cz))
    inv = 1.0 / m[0]
    keep = range(9) if x < 0 else range(18, 27) if x == ROWS else range(27)
    got = pull_back(g, [m[k] * inv for k in (1, 2, 3)], rates, w, keep)
    for q in keep:
        gn[q] = got[q]


def pull_first(x, rates, uck, mb, gn, gy, out):
    lane = lanes()
    first, last = lane == 0, lane == 127
    g = []
    for q, (cx, cy, cz) in enumerate(Q):
        v = gn(x + cx)[q]
        d = x + cx + 2
        if cy == 1:
            v = jnp.where(last, rolly(gy[q], 127 - 8 - d), rolly(v, -1))
        if cy == -1:
            v = jnp.where(first, rolly(gy[q], -d), rolly(v, 1))
        g.append(rollz(v, -cz))
    got = pull_back(g, [uck[x, k] for k in range(3)], rates, mb[field(x + 1, 4)])
    for q in range(27):
        out[q] = got[q]


def exchange(
    sizes, ck_hbm, cot_hbm, wall_hbm, rates_hbm,
    cot, mb, uck, rv, xc, xm, upper, gy, done, beside,
    ck, wall, rates_ref, ey, eh, el, sh, sl, en, ep, load, straight, aslant, send, recv,
):
    nx, ny = sizes
    lane = lanes()

    def device(dx, dy):
        return (
            lax.rem(lax.axis_index("gx") + (dx + nx), nx),
            lax.rem(lax.axis_index("gy") + (dy + ny), ny),
        )

    def signal(sem, dx, steps):
        for dy in steps:
            pl.semaphore_signal(sem, inc=1, device_id=device(dx, dy), device_id_type=MESH)

    place = lax.rem(lax.axis_index("gx"), nx // 2)
    opens, closes = place == 0, place == nx // 2 - 1
    barrier = pltpu.get_barrier_semaphore()
    signal(barrier, -1, (0, 1, -1))

    @pl.when(jnp.logical_not(closes))
    def _():
        signal(barrier, 0, (1, -1))

    loads = []
    for src, dst in ((cot_hbm.reshape(864, 128), cot), (ck_hbm, ck), (wall_hbm, wall), (rates_hbm, rates_ref)):
        loads.append(pltpu.make_async_copy(src, dst, load.at[len(loads)]))
        loads[-1].start()

    @pl.when(closes)
    def _():
        pl.semaphore_wait(barrier, 3)

    @pl.when(jnp.logical_not(closes))
    def _():
        pl.semaphore_wait(barrier, 5)


    copies, late, soon = [], [], []

    def copy_to(src, dst, dx, dy):
        n = len(copies)
        copies.append(
            pltpu.make_async_remote_copy(
                src_ref=src,
                dst_ref=dst,
                send_sem=send.at[n],
                recv_sem=recv.at[n],
                device_id=device(dx, dy),
                device_id_type=MESH,
            )
        )
        (late if dx == 1 else soon).append(copies[-1])
        return copies[-1]

    def put(src, dst, dx, dy):
        copy_to(src, dst, dx, dy).start()

    put(cot_hbm.at[pl.ds(0, 9), :, 3], xc.at[0, pl.ds(0, 9)], 1, 0)
    signal(straight, 1, (0,))
    signal(aslant, 1, (1, -1))
    loads[0].wait()
    for q in range(9):
        sh[q] = row(cot, q + 9, 3)
        sh[q + 9] = row(cot, q, 2)

    zero = jnp.zeros((8, 128), F32)
    first, last = lane == 0, lane == 127
    body = [[zero] * 4 for _ in range(6)]
    edge = [[zero] * 3 for _ in range(6)]
    acc = dict.fromkeys(("r0", "r1", "r2", "l0", "l1", "l2", "l0m"), zero)

    def add(name, v, d):
        acc[name] = jnp.where(lane == d, v, acc[name])

    def pack_cotangent(x):
        for i, (cx, cz) in enumerate([(a, c) for a in range(3) for c in range(3)]):
            d = 8 * i + x + 2
            v = rolly(row(cot, at(cx, 0, cz), x), d - 127)
            add("r0", v, d)
            add("r2", v, d - 1)
            v = rolly(row(cot, at(cx, 2, cz), x), d)
            add("l0", v, d)
            add("l2", v, d + 1)
            v = rolly(row(cot, at(cx, 1, cz), x), d - 127)
            add("r1", v, d)
            add("l1", v, d + 1)

    def pack_sums(r):
        outer = edge[r]
        outer = [outer[0], outer[1], jnp.where(first, outer[0], -outer[0]), outer[2]]
        for k in range(4):
            d = 8 * (9 + k) + r + 1
            v = rolly(body[r][k], d - 127)
            add("r1", v, d)
            add("l1", v, d + 1)
            v = rolly(outer[k], d)
            add("r0", v, d)
            add("l0m", v, d - 1)

    def pack_wall(x, w):
        d = 8 * 13 + x + 2
        v = rolly(w, d - 127)
        add("r1", v, d)
        add("l1", v, d + 1)

    def packed():
        left = acc["l0"] + rolly(acc["l0m"], 1), rolly(acc["l1"], -1), rolly(acc["l2"], -1)
        right = acc["r0"], acc["r1"], rolly(acc["r2"], 1)
        return left, right

    def collide_row(x):
        w = wall_row(wall, x)
        mb[field(x + 1, 4)] = w
        pack_wall(x, w)
        out, u = collide([row(ck, q, x) for q in range(27)], rates, w)
        for k in range(3):
            uck[x, k] = u[k]
        for a in range(3):
            sums, tilts = [], []
            for b in range(3):
                up = rollz(out[at(a, b, 2)], 1)
                down = rollz(out[at(a, b, 0)], -1)
                sums.append(out[at(a, b, 1)] + (up + down))
                tilts.append(up - down)
            ap, am = rolly(sums[2], 1), rolly(sums[0], -1)
            bp, bm = rolly(tilts[2], 1), rolly(tilts[0], -1)
            r = x + a
            outer = jnp.where(first, ap, am)
            edge[r][0] = edge[r][0] + outer
            edge[r][1] = edge[r][1] + (a - 1) * outer if a != 1 else edge[r][1]
            edge[r][2] = edge[r][2] + jnp.where(first, bp, bm)
            ap, am = jnp.where(first, 0.0, ap), jnp.where(last, 0.0, am)
            bp, bm = jnp.where(first, 0.0, bp), jnp.where(last, 0.0, bm)
            total = sums[1] + (ap + am)
            body[r][0] = body[r][0] + total
            if a != 1:
                body[r][1] = body[r][1] + (a - 1) * total
            body[r][2] = body[r][2] + (ap - am)
            body[r][3] = body[r][3] + (tilts[1] + (bp + bm))

    def store_sums(r):
        for k in range(4):
            mb[field(r, k)] = body[r][k]
        pack_sums(r)

    pack_cotangent(3)
    pack_cotangent(2)
    for c in loads[1:]:
        c.wait()
    rates = halved_rates(rates_ref)
    collide_row(3)
    collide_row(2)
    store_sums(5)
    store_sums(4)
    left, right = packed()
    eh[0] = right[0] + (rolly(right[1], -3) + rolly(right[2], 3))
    eh[1] = left[0] + (rolly(left[1], -3) + rolly(left[2], 3))
    eh[2] = left[0] + rolly(right[0], -3)
    put(eh.at[0], ep.at[0], 1, 1)
    put(eh.at[1], ep.at[1], 1, -1)
    put(eh.at[2], ep.at[2], 1, 0)
    put(mb.at[pl.ds(20, 8)], xm.at[0], 1, 0)
    put(sh, xc.at[0, pl.ds(9, 18)], 1, 0)

    pack_cotangent(1)
    pack_cotangent(0)
    collide_row(1)
    collide_row(0)
    for r in range(4):
        store_sums(r)
    left, right = packed()
    for k in range(3):
        ey[k, 0] = left[k]
        ey[k, 1] = right[k]
    rest = (lane % 8 > 0) & (lane % 8 < 4)
    left = [jnp.where(rest, v, 0.0) for v in left]
    right = [jnp.where(rest, v, 0.0) for v in right]
    el[0] = right[0] + (rolly(right[1], 3) + rolly(right[2], 5))
    el[1] = left[0] + (rolly(left[1], 3) + rolly(left[2], 5))
    el[2] = left[0] + rolly(right[0], 3)

    for q in range(18):
        sl[q] = row(cot, q + 9, 0)
    for q in range(9):
        sl[q + 18] = row(cot, q + 18, 1)

    @pl.when(closes)
    def _():
        pl.semaphore_wait(straight, 1)

    put(ey.at[:, 1], en.at[0], 0, 1)
    put(ey.at[:, 0], en.at[1], 0, -1)
    slanting = [
        copy_to(el.at[0], ep.at[3], -1, 1),
        copy_to(el.at[1], ep.at[4], -1, -1),
    ]
    back = [
        copy_to(el.at[2], ep.at[5], -1, 0),
        copy_to(mb.at[pl.ds(2, 8)], xm.at[1], -1, 0),
        copy_to(sl, xc.at[1], -1, 0),
    ]

    @pl.when(jnp.logical_not(opens | closes))
    def _():
        pl.semaphore_wait(straight, 1)

    def send_back():
        for c in back:
            c.start()
        pl.semaphore_wait(aslant, 2)
        for c in slanting:
            c.start()

    @pl.when(jnp.logical_not(opens))
    def _():
        send_back()

    for n in range(27):
        rv[n] = jnp.full((8, 128), rates[n], F32)

    for c in soon:
        c.wait_recv()

    def known(n):
        return rv[n]

    def gn(x):
        return upper.at[x]

    packs = merged(en, ep, ey, False)
    exl, exr = packs[0][0], packs[1][0]
    for x in (4, 3, 2, 1):
        pull_row(x, exl, exr, known, cot, mb, xc, xm, gn(x))
    pull_beside(packs, known, gy)
    for x in (3, 2):
        pull_first(x, known, uck, mb, gn, gy, done.at[x - 1])

    @pl.when(opens)
    def _():
        pl.semaphore_wait(straight, 1)
        send_back()

    for c in late[:-1]:
        c.wait_recv()
    packs = merged(en, ep, ey, True)
    exl, exr = packs[0][0], packs[1][0]
    beside[0], beside[1] = exl, exr
    pull_row(0, exl, exr, known, cot, mb, xc, xm, gn(0))
    pull_beside(packs, known, gy)
    pull_first(1, known, uck, mb, gn, gy, done.at[0])
    late[-1].wait_recv()
    for c in copies:
        c.wait_send()


def finish(cot, mb, uck, rv, xc, xm, upper, gy, done, beside, out, lower, end, sems):
    def rates(n):
        return rv[n]

    def gn(x):
        return lower if x < 0 else upper.at[x]

    copies = []

    def put(src, x):
        copies.append(pltpu.make_async_copy(src, out.at[:, :, x], sems.at[x]))
        copies[-1].start()

    for x in (1, 2, 3):
        put(done.at[x - 1], x)
    pull_row(-1, beside[0], beside[1], rates, cot, mb, xc, xm, lower)
    pull_first(0, rates, uck, mb, gn, gy, end)
    put(end, 0)
    for c in copies:
        c.wait()


def shards(sizes, checkpoint, rates, wall_mask, cotangent):
    ck = checkpoint.reshape(864, 128)
    wall, rates = wall_mask.reshape(32, 128), rates.reshape(1, 27)
    vmem, hbm = pl.BlockSpec(memory_space=pltpu.VMEM), pl.BlockSpec(memory_space=pltpu.HBM)
    small = dict(vmem_limit_bytes=16 << 20)

    def like(*shape):
        return jax.ShapeDtypeStruct(shape, F32)

    got = pl.pallas_call(
        functools.partial(exchange, sizes),
        out_shape=(
            like(864, 128), like(30, 8, 128), like(4, 3, 8, 128), like(27, 8, 128), like(2, 27, 8, 128),
            like(2, 8, 8, 128), like(5, 27, 8, 128), like(27, 8, 128), like(3, 27, 8, 128), like(2, 8, 128),
        ),
        in_specs=[hbm] * 4,
        out_specs=(vmem,) * 10,
        scratch_shapes=[
            pltpu.VMEM((864, 128), F32),
            pltpu.VMEM((32, 128), jnp.int32),
            pltpu.SMEM((1, 27), F32),
            pltpu.VMEM((3, 2, 8, 128), F32),
            pltpu.VMEM((3, 8, 128), F32),
            pltpu.VMEM((3, 8, 128), F32),
            pltpu.VMEM((18, 8, 128), F32),
            pltpu.VMEM((27, 8, 128), F32),
            pltpu.VMEM((2, 3, 8, 128), F32),
            pltpu.VMEM((6, 8, 128), F32),
            pltpu.SemaphoreType.DMA((4,)),
            pltpu.SemaphoreType.REGULAR,
            pltpu.SemaphoreType.REGULAR,
            pltpu.SemaphoreType.DMA((13,)),
            pltpu.SemaphoreType.DMA((13,)),
        ],
        compiler_params=pltpu.CompilerParams(collective_id=0, has_side_effects=True, **small),
        name="exchange",
    )(*[pltpu.with_memory_space_constraint(v, pltpu.HBM) for v in (ck, cotangent, wall, rates)])
    return pl.pallas_call(
        finish,
        out_shape=like(27, 8, 4, 128),
        in_specs=[vmem] * 10,
        out_specs=hbm,
        scratch_shapes=[
            pltpu.VMEM((27, 8, 128), F32),
            pltpu.VMEM((27, 8, 128), F32),
            pltpu.SemaphoreType.DMA((4,)),
        ],
        compiler_params=pltpu.CompilerParams(**small),
        name="finish",
    )(*got)


def solution(mesh):
    sizes = (mesh.shape["gx"], mesh.shape["gy"])
    in_specs = (P(None, None, "gx", "gy"), P(), P(None, "gx", "gy"), P(None, None, "gx", "gy"))
    out_specs = P(None, None, "gx", "gy")
    return jax.shard_map(
        functools.partial(shards, sizes), mesh=mesh, in_specs=in_specs, out_specs=out_specs, check_vma=False
    )
```

```python
import functools

import jax
import jax.numpy as jnp
from jax import lax
from jax.experimental import pallas as pl
from jax.experimental.pallas import tpu as pltpu
from jax.sharding import PartitionSpec as P

F32 = jnp.float32
MESH = pl.DeviceIdType.MESH
ROWS = 4
Q = [(a, b, c) for a in (-1, 0, 1) for b in (-1, 0, 1) for c in (-1, 0, 1)]
THIRD = 1.0 / 3.0
NINTH = 1.0 / 9.0


def rollz(v, s):
    return v if s == 0 else pltpu.roll(v, s % 8, 0)


def rolly(v, s):
    return v if s % 128 == 0 else pltpu.roll(v, s % 128, 1)


def lanes():
    return lax.broadcasted_iota(jnp.int32, (8, 128), 1)


def along(values, axis, fn):
    out = [None] * 27
    step = (9, 3, 1)[axis]
    for i in range(27):
        if (i // step) % 3 == 0:
            out[i], out[i + step], out[i + 2 * step] = fn(
                values[i], values[i + step], values[i + 2 * step]
            )
    return out


def to_moments(a, b, c):
    s = a + c
    return s + b, c - a, s


def from_halved(m0, m1, m2):
    a, c = m2 - m1, m2 + m1
    return a, m0 - (a + c), c


def dual_doubled(a, b, c):
    return b, c - a, (a + c) - (b + b)


def dual_back(m0, m1, m2):
    s = m0 + m2
    return s - m1, m0, s + m1


def at(i, j, k):
    return 9 * i + 3 * j + k


def halved_rates(rates_ref):
    return [
        rates_ref[0, n] * (0.5 ** sum(p > 0 for p in (n // 9, n // 3 % 3, n % 3)))
        for n in range(27)
    ]


def collide(f, rates, wall):
    m = f
    for axis in (2, 1, 0):
        m = along(m, axis, to_moments)
    rho, jx, jy, jz = m[0], m[9], m[3], m[1]
    inv = 1.0 / rho
    ux, uy, uz = jx * inv, jy * inv, jz * inv
    xx, yy, zz = jx * ux, jy * uy, jz * uz
    xy, xz, yz = jx * uy, jx * uz, jy * uz
    r3, r9 = rho * THIRD, rho * NINTH
    x3, y3, z3 = jx * THIRD, jy * THIRD, jz * THIRD
    eq = [None] * 27
    eq[at(0, 0, 0)] = rho
    eq[at(1, 0, 0)], eq[at(0, 1, 0)], eq[at(0, 0, 1)] = jx, jy, jz
    eq[at(2, 0, 0)], eq[at(0, 2, 0)], eq[at(0, 0, 2)] = r3 + xx, r3 + yy, r3 + zz
    eq[at(1, 1, 0)], eq[at(1, 0, 1)], eq[at(0, 1, 1)] = xy, xz, yz
    eq[at(1, 2, 0)] = eq[at(1, 0, 2)] = x3
    eq[at(2, 1, 0)] = eq[at(0, 1, 2)] = y3
    eq[at(2, 0, 1)] = eq[at(0, 2, 1)] = z3
    eq[at(1, 2, 2)], eq[at(2, 1, 2)], eq[at(2, 2, 1)] = x3 * THIRD, y3 * THIRD, z3 * THIRD
    eq[at(1, 1, 2)], eq[at(1, 2, 1)], eq[at(2, 1, 1)] = xy * THIRD, xz * THIRD, yz * THIRD
    eq[at(2, 2, 0)] = r9 + (xx + yy) * THIRD
    eq[at(2, 0, 2)] = r9 + (xx + zz) * THIRD
    eq[at(0, 2, 2)] = r9 + (yy + zz) * THIRD
    eq[at(2, 2, 2)] = r9 * THIRD + (xx + yy + zz) * NINTH
    d = [
        m[n] * rates[n] if eq[n] is None else (m[n] - eq[n]) * rates[n]
        for n in range(27)
    ]
    for axis in (0, 1, 2):
        d = along(d, axis, from_halved)
    solid = wall > 0.5
    out = [jnp.where(solid, f[26 - n], f[n] - d[n]) for n in range(27)]
    return out, (ux, uy, uz)


def pull_back(g, u, rates, wall, keep=range(27)):
    ux, uy, uz = u
    e = g
    for axis in (2, 1, 0):
        e = along(e, axis, dual_doubled)
    e = [e[n] * rates(n) for n in range(27)]
    e222 = e[at(2, 2, 2)] * NINTH
    pair_xy, pair_xz, pair_yz = e[at(2, 2, 0)], e[at(2, 0, 2)], e[at(0, 2, 2)]
    pxx = e[at(2, 0, 0)] + (pair_xy + pair_xz) * THIRD + e222
    pyy = e[at(0, 2, 0)] + (pair_xy + pair_yz) * THIRD + e222
    pzz = e[at(0, 0, 2)] + (pair_xz + pair_yz) * THIRD + e222
    pxy = e[at(1, 1, 0)] + e[at(1, 1, 2)] * THIRD
    pxz = e[at(1, 0, 1)] + e[at(1, 2, 1)] * THIRD
    pyz = e[at(0, 1, 1)] + e[at(2, 1, 1)] * THIRD
    rho = (
        e[0]
        + (e[at(2, 0, 0)] + e[at(0, 2, 0)] + e[at(0, 0, 2)] + e222) * THIRD
        + (pair_xy + pair_xz + pair_yz) * NINTH
    )
    cx = e[at(1, 0, 0)] + (e[at(1, 2, 0)] + e[at(1, 0, 2)]) * THIRD + e[at(1, 2, 2)] * NINTH
    cy = e[at(0, 1, 0)] + (e[at(2, 1, 0)] + e[at(0, 1, 2)]) * THIRD + e[at(2, 1, 2)] * NINTH
    cz = e[at(0, 0, 1)] + (e[at(2, 0, 1)] + e[at(0, 2, 1)]) * THIRD + e[at(2, 2, 1)] * NINTH
    sx = (pxx + pxx) * ux + pxy * uy + pxz * uz
    sy = (pyy + pyy) * uy + pxy * ux + pyz * uz
    sz = (pzz + pzz) * uz + pxz * ux + pyz * uy
    rho = rho - 0.5 * (ux * sx + uy * sy + uz * sz)
    e[at(0, 0, 0)] = e[at(0, 0, 0)] - rho
    e[at(1, 0, 0)] = e[at(1, 0, 0)] - (cx + sx)
    e[at(0, 1, 0)] = e[at(0, 1, 0)] - (cy + sy)
    e[at(0, 0, 1)] = e[at(0, 0, 1)] - (cz + sz)
    for axis in (2, 1, 0):
        e = along(e, axis, dual_back)
    solid = wall > 0.5
    return {n: jnp.where(solid, g[26 - n], g[n] - e[n]) for n in keep}


def row(ref, q, x):
    return ref[pl.ds(q * 32 + x, 8, stride=4), :]


def wall_row(ref, x):
    height = lax.broadcasted_iota(jnp.int32, (8, 128), 0)
    mask = ref[pl.ds(x, 8, stride=4), :]
    return jnp.where((height == 0) | (height == 7), 1, mask).astype(F32)


def merged(en, ep, ey, below):
    lane = lanes() % 8

    def ends(v, k, low):
        if low:
            return jnp.where(lane < (2 if k == 2 else 3), rolly(v, (-4, -1, -7)[k]), 0.0)
        return jnp.where(lane >= (6 if k == 2 else 5), rolly(v, (4, 1, -1)[k]), 0.0)

    def merge(own, k, which):
        own = own + ends(ep[3 + which], k, False)
        return own + ends(ep[which], k, True) if below else own

    exl = [merge(en[0, k], k, 0) for k in range(3)]
    exr = [merge(en[1, k], k, 1) for k in range(3)]
    oxl = merge(ey[0, 0], 0, 2)
    oxr = merge(ey[0, 1], 1, 2)
    return exl, exr, oxl, oxr


def field(r, k):
    if r == 0:
        return {0: 2, 2: 3, 3: 4, 1: 0, 4: 1}[k]
    return 5 * r + {0: 0, 2: 1, 3: 2, 1: 3, 4: 4}[k]


def slot(q):
    return 3 * (q // 9) + q % 3


def pull_beside(packs, rates, gy):
    exl, exr, oxl, oxr = packs
    lane = lanes()
    left = lane < 8
    g = []
    for q, (cx, cy, cz) in enumerate(Q):
        s = slot(q)
        lo, hi = ((exl[2], oxr), (exl[1], exr[1]), (oxl, exr[2]))[cy + 1]
        v = jnp.where(left, rolly(lo, -8 * s - cx), rolly(hi, 8 - 8 * s - cx))
        g.append(rollz(v, -cz))
    m = []
    lo, hi = exl[1] + oxl, exr[1] + oxr
    for k in range(4):
        s = 9 + k
        m.append(jnp.where(left, rolly(lo, -8 * s), rolly(hi, 8 - 8 * s)))
    w = jnp.where(left, rolly(exl[1], -104), rolly(exr[1], -96))
    inv = 1.0 / jnp.where(m[0] > 0.0, m[0], 1.0)
    got = pull_back(g, [m[k] * inv for k in (1, 2, 3)], rates, w)
    for q, (cx, cy, cz) in enumerate(Q):
        if cy != 0:
            gy[q] = got[q]


def pull_row(x, exl, exr, rates, cot, mb, xc, xm, gn):
    lane = lanes()
    first, last = lane == 0, lane == 127

    def source(q, x):
        if 0 <= x < ROWS:
            return row(cot, q, x)
        if x == -1:
            return xc[0, q]
        if x == -2:
            return xc[0, 18 + q]
        return xc[1, q - 9] if x == ROWS else xc[1, q]

    m = []
    for k in range(4):
        v = mb[field(x + 1, k)]
        if x == -1:
            v = v + xm[0, field(1, k) - 5]
        if x == 0:
            v = v + xm[0, field(1, 0 if k == 1 else k)]
        if x == 3:
            v = v - xm[1, 0] if k == 1 else v + xm[1, field(0, k) - 2]
        if x == 4:
            v = v + xm[1, field(1, k) - 2]
        d = 8 * (9 + k) + x + 2
        v = v + jnp.where(first, rolly(exl, -d), 0.0)
        v = v + jnp.where(last, rolly(exr, 127 - d), 0.0)
        m.append(v)
    w = xm[0, 4] if x < 0 else xm[1, 7] if x == ROWS else mb[field(x + 1, 4)]
    g = []
    for q, (cx, cy, cz) in enumerate(Q):
        v = source(q, x + cx)
        d = 8 * slot(q) + x + cx + 2
        if cy == 1:
            v = jnp.where(last, rolly(exr, 127 - d), rolly(v, -1))
        if cy == -1:
            v = jnp.where(first, rolly(exl, -d), rolly(v, 1))
        g.append(rollz(v, -cz))
    inv = 1.0 / m[0]
    keep = range(9) if x < 0 else range(18, 27) if x == ROWS else range(27)
    got = pull_back(g, [m[k] * inv for k in (1, 2, 3)], rates, w, keep)
    for q in keep:
        gn[q] = got[q]


def pull_first(x, rates, uck, mb, gn, gy, out):
    lane = lanes()
    first, last = lane == 0, lane == 127
    g = []
    for q, (cx, cy, cz) in enumerate(Q):
        v = gn(x + cx)[q]
        d = x + cx + 2
        if cy == 1:
            v = jnp.where(last, rolly(gy[q], 127 - 8 - d), rolly(v, -1))
        if cy == -1:
            v = jnp.where(first, rolly(gy[q], -d), rolly(v, 1))
        g.append(rollz(v, -cz))
    got = pull_back(g, [uck[x, k] for k in range(3)], rates, mb[field(x + 1, 4)])
    for q in range(27):
        out[q] = got[q]


def exchange(
    sizes, ck_hbm, cot_hbm, wall_hbm, rates_hbm,
    cot, mb, uck, rv, xc, xm, upper, gy, done, beside,
    ck, wall, rates_ref, ey, eh, el, sh, sl, en, ep, load, straight, aslant, send, recv,
):
    nx, ny = sizes
    lane = lanes()

    def device(dx, dy):
        return (
            lax.rem(lax.axis_index("gx") + (dx + nx), nx),
            lax.rem(lax.axis_index("gy") + (dy + ny), ny),
        )

    def signal(sem, dx, steps):
        for dy in steps:
            pl.semaphore_signal(sem, inc=1, device_id=device(dx, dy), device_id_type=MESH)

    loads = []
    for src, dst in (
        (cot_hbm.at[pl.ds(0, 18), :, 3], sh.at[pl.ds(0, 18)]),
        (cot_hbm.at[pl.ds(0, 9), :, 2], sh.at[pl.ds(18, 9)]),
        (ck_hbm.at[:, :, 3], ck.at[3]),
        (ck_hbm.at[:, :, 2], ck.at[2]),
        (wall_hbm, wall),
        (rates_hbm, rates_ref),
        (cot_hbm.reshape(864, 128), cot),
        (ck_hbm.at[:, :, 1], ck.at[1]),
        (ck_hbm.at[:, :, 0], ck.at[0]),
    ):
        loads.append(pltpu.make_async_copy(src, dst, load.at[len(loads)]))
        loads[-1].start()

    place = lax.rem(lax.axis_index("gx"), nx // 2)
    opens, closes = place == 0, place == nx // 2 - 1
    barrier = pltpu.get_barrier_semaphore()
    signal(barrier, -1, (0, 1, -1))

    @pl.when(jnp.logical_not(closes))
    def _():
        signal(barrier, 0, (1, -1))

    @pl.when(closes)
    def _():
        pl.semaphore_wait(barrier, 3)

    @pl.when(jnp.logical_not(closes))
    def _():
        pl.semaphore_wait(barrier, 5)


    copies, late, soon = [], [], []

    def copy_to(src, dst, dx, dy):
        n = len(copies)
        copies.append(
            pltpu.make_async_remote_copy(
                src_ref=src,
                dst_ref=dst,
                send_sem=send.at[n],
                recv_sem=recv.at[n],
                device_id=device(dx, dy),
                device_id_type=MESH,
            )
        )
        (late if dx == 1 else soon).append(copies[-1])
        return copies[-1]

    def put(src, dst, dx, dy):
        copy_to(src, dst, dx, dy).start()

    put(cot_hbm.at[pl.ds(0, 9), :, 3], xc.at[0, pl.ds(0, 9)], 1, 0)
    signal(straight, 1, (0,))
    signal(aslant, 1, (1, -1))
    zero = jnp.zeros((8, 128), F32)
    first, last = lane == 0, lane == 127
    body = [[zero] * 4 for _ in range(6)]
    edge = [[zero] * 3 for _ in range(6)]
    acc = dict.fromkeys(("r0", "r1", "r2", "l0", "l1", "l2", "l0m"), zero)

    def add(name, v, d):
        acc[name] = jnp.where(lane == d, v, acc[name])

    def pack_cotangent(x, steps, get):
        for cx, cz in [(a, c) for a in steps for c in range(3)]:
            d = 8 * (3 * cx + cz) + x + 2
            v = rolly(get(at(cx, 0, cz)), d - 127)
            add("r0", v, d)
            add("r2", v, d - 1)
            v = rolly(get(at(cx, 2, cz)), d)
            add("l0", v, d)
            add("l2", v, d + 1)
            v = rolly(get(at(cx, 1, cz)), d - 127)
            add("r1", v, d)
            add("l1", v, d + 1)

    def pack_sums(r):
        outer = edge[r]
        outer = [outer[0], outer[1], jnp.where(first, outer[0], -outer[0]), outer[2]]
        for k in range(4):
            d = 8 * (9 + k) + r + 1
            v = rolly(body[r][k], d - 127)
            add("r1", v, d)
            add("l1", v, d + 1)
            v = rolly(outer[k], d)
            add("r0", v, d)
            add("l0m", v, d - 1)

    def pack_wall(x, w):
        d = 8 * 13 + x + 2
        v = rolly(w, d - 127)
        add("r1", v, d)
        add("l1", v, d + 1)

    def packed():
        left = acc["l0"] + rolly(acc["l0m"], 1), rolly(acc["l1"], -1), rolly(acc["l2"], -1)
        right = acc["r0"], acc["r1"], rolly(acc["r2"], 1)
        return left, right

    def collide_row(x):
        w = wall_row(wall, x)
        mb[field(x + 1, 4)] = w
        pack_wall(x, w)
        out, u = collide([ck[x, q] for q in range(27)], rates, w)
        for k in range(3):
            uck[x, k] = u[k]
        for a in range(3):
            sums, tilts = [], []
            for b in range(3):
                up = rollz(out[at(a, b, 2)], 1)
                down = rollz(out[at(a, b, 0)], -1)
                sums.append(out[at(a, b, 1)] + (up + down))
                tilts.append(up - down)
            ap, am = rolly(sums[2], 1), rolly(sums[0], -1)
            bp, bm = rolly(tilts[2], 1), rolly(tilts[0], -1)
            r = x + a
            outer = jnp.where(first, ap, am)
            edge[r][0] = edge[r][0] + outer
            edge[r][1] = edge[r][1] + (a - 1) * outer if a != 1 else edge[r][1]
            edge[r][2] = edge[r][2] + jnp.where(first, bp, bm)
            ap, am = jnp.where(first, 0.0, ap), jnp.where(last, 0.0, am)
            bp, bm = jnp.where(first, 0.0, bp), jnp.where(last, 0.0, bm)
            total = sums[1] + (ap + am)
            body[r][0] = body[r][0] + total
            if a != 1:
                body[r][1] = body[r][1] + (a - 1) * total
            body[r][2] = body[r][2] + (ap - am)
            body[r][3] = body[r][3] + (tilts[1] + (bp + bm))

    def store_sums(r):
        for k in range(4):
            mb[field(r, k)] = body[r][k]
        pack_sums(r)

    for c in loads[:6]:
        c.wait()
    pack_cotangent(3, (0, 1), lambda q: sh[q])
    pack_cotangent(2, (0,), lambda q: sh[q + 18])
    rates = halved_rates(rates_ref)
    collide_row(3)
    collide_row(2)
    store_sums(5)
    store_sums(4)
    left, right = packed()
    eh[0] = right[0] + (rolly(right[1], -3) + rolly(right[2], 3))
    eh[1] = left[0] + (rolly(left[1], -3) + rolly(left[2], 3))
    eh[2] = left[0] + rolly(right[0], -3)
    put(eh.at[0], ep.at[0], 1, 1)
    put(eh.at[1], ep.at[1], 1, -1)
    put(eh.at[2], ep.at[2], 1, 0)
    put(mb.at[pl.ds(20, 8)], xm.at[0], 1, 0)
    put(sh.at[pl.ds(9, 18)], xc.at[0, pl.ds(9, 18)], 1, 0)

    for c in loads[6:]:
        c.wait()
    for x, steps in ((3, (2,)), (2, (1, 2)), (1, range(3)), (0, range(3))):
        pack_cotangent(x, steps, lambda q: row(cot, q, x))
    collide_row(1)
    collide_row(0)
    for r in range(4):
        store_sums(r)
    left, right = packed()
    for k in range(3):
        ey[k, 0] = left[k]
        ey[k, 1] = right[k]
    rest = (lane % 8 > 0) & (lane % 8 < 4)
    left = [jnp.where(rest, v, 0.0) for v in left]
    right = [jnp.where(rest, v, 0.0) for v in right]
    el[0] = right[0] + (rolly(right[1], 3) + rolly(right[2], 5))
    el[1] = left[0] + (rolly(left[1], 3) + rolly(left[2], 5))
    el[2] = left[0] + rolly(right[0], 3)

    for q in range(18):
        sl[q] = row(cot, q + 9, 0)
    for q in range(9):
        sl[q + 18] = row(cot, q + 18, 1)

    @pl.when(closes)
    def _():
        pl.semaphore_wait(straight, 1)

    put(ey.at[:, 1], en.at[0], 0, 1)
    put(ey.at[:, 0], en.at[1], 0, -1)
    slanting = [
        copy_to(el.at[0], ep.at[3], -1, 1),
        copy_to(el.at[1], ep.at[4], -1, -1),
    ]
    back = [
        copy_to(el.at[2], ep.at[5], -1, 0),
        copy_to(mb.at[pl.ds(2, 8)], xm.at[1], -1, 0),
        copy_to(sl, xc.at[1], -1, 0),
    ]

    @pl.when(jnp.logical_not(opens | closes))
    def _():
        pl.semaphore_wait(straight, 1)

    def send_back():
        for c in back:
            c.start()
        pl.semaphore_wait(aslant, 2)
        for c in slanting:
            c.start()

    @pl.when(jnp.logical_not(opens))
    def _():
        send_back()

    for n in range(27):
        rv[n] = jnp.full((8, 128), rates[n], F32)

    for c in soon:
        c.wait_recv()

    def known(n):
        return rv[n]

    def gn(x):
        return upper.at[x]

    packs = merged(en, ep, ey, False)
    exl, exr = packs[0][0], packs[1][0]
    for x in (4, 3, 2, 1):
        pull_row(x, exl, exr, known, cot, mb, xc, xm, gn(x))
    pull_beside(packs, known, gy)
    for x in (3, 2):
        pull_first(x, known, uck, mb, gn, gy, done.at[x - 1])

    @pl.when(opens)
    def _():
        pl.semaphore_wait(straight, 1)
        send_back()

    for c in late[:-1]:
        c.wait_recv()
    packs = merged(en, ep, ey, True)
    exl, exr = packs[0][0], packs[1][0]
    beside[0], beside[1] = exl, exr
    pull_row(0, exl, exr, known, cot, mb, xc, xm, gn(0))
    pull_beside(packs, known, gy)
    pull_first(1, known, uck, mb, gn, gy, done.at[0])
    late[-1].wait_recv()
    for c in copies:
        c.wait_send()


def finish(cot, mb, uck, rv, xc, xm, upper, gy, done, beside, out, lower, end, sems):
    def rates(n):
        return rv[n]

    def gn(x):
        return lower if x < 0 else upper.at[x]

    copies = []

    def put(src, x):
        copies.append(pltpu.make_async_copy(src, out.at[:, :, x], sems.at[x]))
        copies[-1].start()

    for x in (1, 2, 3):
        put(done.at[x - 1], x)
    pull_row(-1, beside[0], beside[1], rates, cot, mb, xc, xm, lower)
    pull_first(0, rates, uck, mb, gn, gy, end)
    put(end, 0)
    for c in copies:
        c.wait()


def shards(sizes, checkpoint, rates, wall_mask, cotangent):
    wall, rates = wall_mask.reshape(32, 128), rates.reshape(1, 27)
    vmem, hbm = pl.BlockSpec(memory_space=pltpu.VMEM), pl.BlockSpec(memory_space=pltpu.HBM)
    small = dict(vmem_limit_bytes=16 << 20)

    def like(*shape):
        return jax.ShapeDtypeStruct(shape, F32)

    got = pl.pallas_call(
        functools.partial(exchange, sizes),
        out_shape=(
            like(864, 128), like(30, 8, 128), like(4, 3, 8, 128), like(27, 8, 128), like(2, 27, 8, 128),
            like(2, 8, 8, 128), like(5, 27, 8, 128), like(27, 8, 128), like(3, 27, 8, 128), like(2, 8, 128),
        ),
        in_specs=[hbm] * 4,
        out_specs=(vmem,) * 10,
        scratch_shapes=[
            pltpu.VMEM((4, 27, 8, 128), F32),
            pltpu.VMEM((32, 128), jnp.int32),
            pltpu.SMEM((1, 27), F32),
            pltpu.VMEM((3, 2, 8, 128), F32),
            pltpu.VMEM((3, 8, 128), F32),
            pltpu.VMEM((3, 8, 128), F32),
            pltpu.VMEM((27, 8, 128), F32),
            pltpu.VMEM((27, 8, 128), F32),
            pltpu.VMEM((2, 3, 8, 128), F32),
            pltpu.VMEM((6, 8, 128), F32),
            pltpu.SemaphoreType.DMA((9,)),
            pltpu.SemaphoreType.REGULAR,
            pltpu.SemaphoreType.REGULAR,
            pltpu.SemaphoreType.DMA((13,)),
            pltpu.SemaphoreType.DMA((13,)),
        ],
        compiler_params=pltpu.CompilerParams(collective_id=0, has_side_effects=True, **small),
        name="exchange",
    )(*[pltpu.with_memory_space_constraint(v, pltpu.HBM) for v in (checkpoint, cotangent, wall, rates)])
    return pl.pallas_call(
        finish,
        out_shape=like(27, 8, 4, 128),
        in_specs=[vmem] * 10,
        out_specs=hbm,
        scratch_shapes=[
            pltpu.VMEM((27, 8, 128), F32),
            pltpu.VMEM((27, 8, 128), F32),
            pltpu.SemaphoreType.DMA((4,)),
        ],
        compiler_params=pltpu.CompilerParams(**small),
        name="finish",
    )(*got)


def solution(mesh):
    sizes = (mesh.shape["gx"], mesh.shape["gy"])
    in_specs = (P(None, None, "gx", "gy"), P(), P(None, "gx", "gy"), P(None, None, "gx", "gy"))
    out_specs = P(None, None, "gx", "gy")
    return jax.shard_map(
        functools.partial(shards, sizes), mesh=mesh, in_specs=in_specs, out_specs=out_specs, check_vma=False
    )
```

```python
import functools

import jax
import jax.numpy as jnp
from jax import lax
from jax.experimental import pallas as pl
from jax.experimental.pallas import tpu as pltpu
from jax.sharding import PartitionSpec as P

F32 = jnp.float32
MESH = pl.DeviceIdType.MESH
ROWS = 4
Q = [(a, b, c) for a in (-1, 0, 1) for b in (-1, 0, 1) for c in (-1, 0, 1)]
THIRD = 1.0 / 3.0
NINTH = 1.0 / 9.0


def rollz(v, s):
    return v if s == 0 else pltpu.roll(v, s % 8, 0)


def rolly(v, s):
    return v if s % 128 == 0 else pltpu.roll(v, s % 128, 1)


def lanes():
    return lax.broadcasted_iota(jnp.int32, (8, 128), 1)


def along(values, axis, fn):
    out = [None] * 27
    step = (9, 3, 1)[axis]
    for i in range(27):
        if (i // step) % 3 == 0:
            out[i], out[i + step], out[i + 2 * step] = fn(
                values[i], values[i + step], values[i + 2 * step]
            )
    return out


def to_moments(a, b, c):
    s = a + c
    return s + b, c - a, s


def from_halved(m0, m1, m2):
    a, c = m2 - m1, m2 + m1
    return a, m0 - (a + c), c


def dual_doubled(a, b, c):
    return b, c - a, (a + c) - (b + b)


def dual_back(m0, m1, m2):
    s = m0 + m2
    return s - m1, m0, s + m1


def at(i, j, k):
    return 9 * i + 3 * j + k


def halved_rates(rates_ref):
    return [
        rates_ref[0, n] * (0.5 ** sum(p > 0 for p in (n // 9, n // 3 % 3, n % 3)))
        for n in range(27)
    ]


def collide(f, rates, wall):
    m = f
    for axis in (2, 1, 0):
        m = along(m, axis, to_moments)
    rho, jx, jy, jz = m[0], m[9], m[3], m[1]
    inv = 1.0 / rho
    ux, uy, uz = jx * inv, jy * inv, jz * inv
    xx, yy, zz = jx * ux, jy * uy, jz * uz
    xy, xz, yz = jx * uy, jx * uz, jy * uz
    r3, r9 = rho * THIRD, rho * NINTH
    x3, y3, z3 = jx * THIRD, jy * THIRD, jz * THIRD
    eq = [None] * 27
    eq[at(0, 0, 0)] = rho
    eq[at(1, 0, 0)], eq[at(0, 1, 0)], eq[at(0, 0, 1)] = jx, jy, jz
    eq[at(2, 0, 0)], eq[at(0, 2, 0)], eq[at(0, 0, 2)] = r3 + xx, r3 + yy, r3 + zz
    eq[at(1, 1, 0)], eq[at(1, 0, 1)], eq[at(0, 1, 1)] = xy, xz, yz
    eq[at(1, 2, 0)] = eq[at(1, 0, 2)] = x3
    eq[at(2, 1, 0)] = eq[at(0, 1, 2)] = y3
    eq[at(2, 0, 1)] = eq[at(0, 2, 1)] = z3
    eq[at(1, 2, 2)], eq[at(2, 1, 2)], eq[at(2, 2, 1)] = x3 * THIRD, y3 * THIRD, z3 * THIRD
    eq[at(1, 1, 2)], eq[at(1, 2, 1)], eq[at(2, 1, 1)] = xy * THIRD, xz * THIRD, yz * THIRD
    eq[at(2, 2, 0)] = r9 + (xx + yy) * THIRD
    eq[at(2, 0, 2)] = r9 + (xx + zz) * THIRD
    eq[at(0, 2, 2)] = r9 + (yy + zz) * THIRD
    eq[at(2, 2, 2)] = r9 * THIRD + (xx + yy + zz) * NINTH
    d = [
        m[n] * rates[n] if eq[n] is None else (m[n] - eq[n]) * rates[n]
        for n in range(27)
    ]
    for axis in (0, 1, 2):
        d = along(d, axis, from_halved)
    solid = wall > 0.5
    out = [jnp.where(solid, f[26 - n], f[n] - d[n]) for n in range(27)]
    return out, (ux, uy, uz)


def pull_back(g, u, rates, wall, keep=range(27)):
    ux, uy, uz = u
    e = g
    for axis in (2, 1, 0):
        e = along(e, axis, dual_doubled)
    e = [e[n] * rates(n) for n in range(27)]
    e222 = e[at(2, 2, 2)] * NINTH
    pair_xy, pair_xz, pair_yz = e[at(2, 2, 0)], e[at(2, 0, 2)], e[at(0, 2, 2)]
    pxx = e[at(2, 0, 0)] + (pair_xy + pair_xz) * THIRD + e222
    pyy = e[at(0, 2, 0)] + (pair_xy + pair_yz) * THIRD + e222
    pzz = e[at(0, 0, 2)] + (pair_xz + pair_yz) * THIRD + e222
    pxy = e[at(1, 1, 0)] + e[at(1, 1, 2)] * THIRD
    pxz = e[at(1, 0, 1)] + e[at(1, 2, 1)] * THIRD
    pyz = e[at(0, 1, 1)] + e[at(2, 1, 1)] * THIRD
    rho = (
        e[0]
        + (e[at(2, 0, 0)] + e[at(0, 2, 0)] + e[at(0, 0, 2)] + e222) * THIRD
        + (pair_xy + pair_xz + pair_yz) * NINTH
    )
    cx = e[at(1, 0, 0)] + (e[at(1, 2, 0)] + e[at(1, 0, 2)]) * THIRD + e[at(1, 2, 2)] * NINTH
    cy = e[at(0, 1, 0)] + (e[at(2, 1, 0)] + e[at(0, 1, 2)]) * THIRD + e[at(2, 1, 2)] * NINTH
    cz = e[at(0, 0, 1)] + (e[at(2, 0, 1)] + e[at(0, 2, 1)]) * THIRD + e[at(2, 2, 1)] * NINTH
    sx = (pxx + pxx) * ux + pxy * uy + pxz * uz
    sy = (pyy + pyy) * uy + pxy * ux + pyz * uz
    sz = (pzz + pzz) * uz + pxz * ux + pyz * uy
    rho = rho - 0.5 * (ux * sx + uy * sy + uz * sz)
    e[at(0, 0, 0)] = e[at(0, 0, 0)] - rho
    e[at(1, 0, 0)] = e[at(1, 0, 0)] - (cx + sx)
    e[at(0, 1, 0)] = e[at(0, 1, 0)] - (cy + sy)
    e[at(0, 0, 1)] = e[at(0, 0, 1)] - (cz + sz)
    for axis in (2, 1, 0):
        e = along(e, axis, dual_back)
    solid = wall > 0.5
    return {n: jnp.where(solid, g[26 - n], g[n] - e[n]) for n in keep}


def row(ref, q, x):
    return ref[pl.ds(q * 32 + x, 8, stride=4), :]


def wall_row(ref, x):
    height = lax.broadcasted_iota(jnp.int32, (8, 128), 0)
    mask = ref[pl.ds(x, 8, stride=4), :]
    return jnp.where((height == 0) | (height == 7), 1, mask).astype(F32)


def merged(en, ep, ey, below):
    lane = lanes() % 8

    def ends(v, k, low):
        if low:
            return jnp.where(lane < (2 if k == 2 else 3), rolly(v, (-4, -1, -7)[k]), 0.0)
        return jnp.where(lane >= (6 if k == 2 else 5), rolly(v, (4, 1, -1)[k]), 0.0)

    def merge(own, k, which):
        own = own + ends(ep[3 + which], k, False)
        return own + ends(ep[which], k, True) if below else own

    exl = [merge(en[0, k], k, 0) for k in range(3)]
    exr = [merge(en[1, k], k, 1) for k in range(3)]
    oxl = merge(ey[0, 0], 0, 2)
    oxr = merge(ey[0, 1], 1, 2)
    return exl, exr, oxl, oxr


def field(r, k):
    if r == 0:
        return {0: 2, 2: 3, 3: 4, 1: 0, 4: 1}[k]
    return 5 * r + {0: 0, 2: 1, 3: 2, 1: 3, 4: 4}[k]


def slot(q):
    return 3 * (q // 9) + q % 3


def pull_beside(packs, rates, gy):
    exl, exr, oxl, oxr = packs
    lane = lanes()
    left = lane < 8
    g = []
    for q, (cx, cy, cz) in enumerate(Q):
        s = slot(q)
        lo, hi = ((exl[2], oxr), (exl[1], exr[1]), (oxl, exr[2]))[cy + 1]
        v = jnp.where(left, rolly(lo, -8 * s - cx), rolly(hi, 8 - 8 * s - cx))
        g.append(rollz(v, -cz))
    m = []
    lo, hi = exl[1] + oxl, exr[1] + oxr
    for k in range(4):
        s = 9 + k
        m.append(jnp.where(left, rolly(lo, -8 * s), rolly(hi, 8 - 8 * s)))
    w = jnp.where(left, rolly(exl[1], -104), rolly(exr[1], -96))
    cell = (lane < 16) & (lane % 8 > 0) & (lane % 8 < 7)
    inv = 1.0 / jnp.where(cell, m[0], 1.0)
    got = pull_back(g, [m[k] * inv for k in (1, 2, 3)], rates, w)
    for q, (cx, cy, cz) in enumerate(Q):
        if cy != 0:
            gy[q] = got[q]


def pull_row(x, exl, exr, rates, cot, mb, xc, xm, gn):
    lane = lanes()
    first, last = lane == 0, lane == 127

    def source(q, x):
        if 0 <= x < ROWS:
            return row(cot, q, x)
        if x == -1:
            return xc[0, q]
        if x == -2:
            return xc[0, 18 + q]
        return xc[1, q - 9] if x == ROWS else xc[1, q]

    m = []
    for k in range(4):
        v = mb[field(x + 1, k)]
        if x == -1:
            v = v + xm[0, field(1, k) - 5]
        if x == 0:
            v = v + xm[0, field(1, 0 if k == 1 else k)]
        if x == 3:
            v = v - xm[1, 0] if k == 1 else v + xm[1, field(0, k) - 2]
        if x == 4:
            v = v + xm[1, field(1, k) - 2]
        d = 8 * (9 + k) + x + 2
        v = v + jnp.where(first, rolly(exl, -d), 0.0)
        v = v + jnp.where(last, rolly(exr, 127 - d), 0.0)
        m.append(v)
    w = xm[0, 4] if x < 0 else xm[1, 7] if x == ROWS else mb[field(x + 1, 4)]
    g = []
    for q, (cx, cy, cz) in enumerate(Q):
        v = source(q, x + cx)
        d = 8 * slot(q) + x + cx + 2
        if cy == 1:
            v = jnp.where(last, rolly(exr, 127 - d), rolly(v, -1))
        if cy == -1:
            v = jnp.where(first, rolly(exl, -d), rolly(v, 1))
        g.append(rollz(v, -cz))
    inv = 1.0 / m[0]
    keep = range(9) if x < 0 else range(18, 27) if x == ROWS else range(27)
    got = pull_back(g, [m[k] * inv for k in (1, 2, 3)], rates, w, keep)
    for q in keep:
        gn[q] = got[q]


def pull_first(x, rates, uck, mb, gn, gy, out):
    lane = lanes()
    first, last = lane == 0, lane == 127
    g = []
    for q, (cx, cy, cz) in enumerate(Q):
        v = gn(x + cx)[q]
        d = x + cx + 2
        if cy == 1:
            v = jnp.where(last, rolly(gy[q], 127 - 8 - d), rolly(v, -1))
        if cy == -1:
            v = jnp.where(first, rolly(gy[q], -d), rolly(v, 1))
        g.append(rollz(v, -cz))
    got = pull_back(g, [uck[x, k] for k in range(3)], rates, mb[field(x + 1, 4)])
    for q in range(27):
        out[q] = got[q]


def exchange(
    sizes, ck_hbm, cot_hbm, wall_hbm, rates_hbm,
    cot, mb, uck, rv, xc, xm, upper, gy, done, beside,
    ck, wall, rates_ref, ey, eh, el, sh, sl, en, ep, load, straight, aslant, send, recv,
):
    nx, ny = sizes
    lane = lanes()

    def device(dx, dy):
        return (
            lax.rem(lax.axis_index("gx") + (dx + nx), nx),
            lax.rem(lax.axis_index("gy") + (dy + ny), ny),
        )

    def signal(sem, dx, steps):
        for dy in steps:
            pl.semaphore_signal(sem, inc=1, device_id=device(dx, dy), device_id_type=MESH)

    loads = []
    for src, dst in (
        (rates_hbm, rates_ref),
        (wall_hbm, wall),
        (ck_hbm.at[:, :, 3], ck.at[3]),
        (ck_hbm.at[:, :, 2], ck.at[2]),
        (cot_hbm.at[pl.ds(0, 18), :, 3], sh.at[pl.ds(0, 18)]),
        (cot_hbm.at[pl.ds(0, 9), :, 2], sh.at[pl.ds(18, 9)]),
        (cot_hbm.reshape(864, 128), cot),
        (ck_hbm.at[:, :, 1], ck.at[1]),
        (ck_hbm.at[:, :, 0], ck.at[0]),
    ):
        loads.append(pltpu.make_async_copy(src, dst, load.at[len(loads)]))
        loads[-1].start()

    place = lax.rem(lax.axis_index("gx"), nx // 2)
    opens, closes = place == 0, place == nx // 2 - 1
    barrier = pltpu.get_barrier_semaphore()
    signal(barrier, -1, (0, 1, -1))

    @pl.when(jnp.logical_not(closes))
    def _():
        signal(barrier, 0, (1, -1))

    @pl.when(closes)
    def _():
        pl.semaphore_wait(barrier, 3)

    @pl.when(jnp.logical_not(closes))
    def _():
        pl.semaphore_wait(barrier, 5)


    copies, late, soon = [], [], []

    def copy_to(src, dst, dx, dy):
        n = len(copies)
        copies.append(
            pltpu.make_async_remote_copy(
                src_ref=src,
                dst_ref=dst,
                send_sem=send.at[n],
                recv_sem=recv.at[n],
                device_id=device(dx, dy),
                device_id_type=MESH,
            )
        )
        (late if dx == 1 else soon).append(copies[-1])
        return copies[-1]

    def put(src, dst, dx, dy):
        copy_to(src, dst, dx, dy).start()

    put(cot_hbm.at[pl.ds(0, 9), :, 3], xc.at[0, pl.ds(0, 9)], 1, 0)
    signal(straight, 1, (0,))
    signal(aslant, 1, (1, -1))
    zero = jnp.zeros((8, 128), F32)
    first, last = lane == 0, lane == 127
    body = [[zero] * 4 for _ in range(6)]
    edge = [[zero] * 3 for _ in range(6)]
    acc = dict.fromkeys(("r0", "r1", "r2", "l0", "l1", "l2", "l0m"), zero)

    def add(name, v, d):
        acc[name] = jnp.where(lane == d, v, acc[name])

    def pack_cotangent(x, steps, get):
        for cx, cz in [(a, c) for a in steps for c in range(3)]:
            d = 8 * (3 * cx + cz) + x + 2
            v = rolly(get(at(cx, 0, cz)), d - 127)
            add("r0", v, d)
            add("r2", v, d - 1)
            v = rolly(get(at(cx, 2, cz)), d)
            add("l0", v, d)
            add("l2", v, d + 1)
            v = rolly(get(at(cx, 1, cz)), d - 127)
            add("r1", v, d)
            add("l1", v, d + 1)

    def pack_sums(r):
        outer = edge[r]
        outer = [outer[0], outer[1], jnp.where(first, outer[0], -outer[0]), outer[2]]
        for k in range(4):
            d = 8 * (9 + k) + r + 1
            v = rolly(body[r][k], d - 127)
            add("r1", v, d)
            add("l1", v, d + 1)
            v = rolly(outer[k], d)
            add("r0", v, d)
            add("l0m", v, d - 1)

    def pack_wall(x, w):
        d = 8 * 13 + x + 2
        v = rolly(w, d - 127)
        add("r1", v, d)
        add("l1", v, d + 1)

    def packed():
        left = acc["l0"] + rolly(acc["l0m"], 1), rolly(acc["l1"], -1), rolly(acc["l2"], -1)
        right = acc["r0"], acc["r1"], rolly(acc["r2"], 1)
        return left, right

    def collide_row(x):
        w = wall_row(wall, x)
        mb[field(x + 1, 4)] = w
        pack_wall(x, w)
        out, u = collide([ck[x, q] for q in range(27)], rates, w)
        for k in range(3):
            uck[x, k] = u[k]
        for a in range(3):
            sums, tilts = [], []
            for b in range(3):
                up = rollz(out[at(a, b, 2)], 1)
                down = rollz(out[at(a, b, 0)], -1)
                sums.append(out[at(a, b, 1)] + (up + down))
                tilts.append(up - down)
            ap, am = rolly(sums[2], 1), rolly(sums[0], -1)
            bp, bm = rolly(tilts[2], 1), rolly(tilts[0], -1)
            r = x + a
            outer = jnp.where(first, ap, am)
            edge[r][0] = edge[r][0] + outer
            edge[r][1] = edge[r][1] + (a - 1) * outer if a != 1 else edge[r][1]
            edge[r][2] = edge[r][2] + jnp.where(first, bp, bm)
            ap, am = jnp.where(first, 0.0, ap), jnp.where(last, 0.0, am)
            bp, bm = jnp.where(first, 0.0, bp), jnp.where(last, 0.0, bm)
            total = sums[1] + (ap + am)
            body[r][0] = body[r][0] + total
            if a != 1:
                body[r][1] = body[r][1] + (a - 1) * total
            body[r][2] = body[r][2] + (ap - am)
            body[r][3] = body[r][3] + (tilts[1] + (bp + bm))

    def store_sums(r):
        for k in range(4):
            mb[field(r, k)] = body[r][k]
        pack_sums(r)

    for c in loads[:6]:
        c.wait()
    pack_cotangent(3, (0, 1), lambda q: sh[q])
    pack_cotangent(2, (0,), lambda q: sh[q + 18])
    rates = halved_rates(rates_ref)
    collide_row(3)
    collide_row(2)
    store_sums(5)
    store_sums(4)
    left, right = packed()
    eh[0] = right[0] + (rolly(right[1], -3) + rolly(right[2], 3))
    eh[1] = left[0] + (rolly(left[1], -3) + rolly(left[2], 3))
    eh[2] = left[0] + rolly(right[0], -3)
    put(eh.at[1], ep.at[1], 1, -1)
    put(eh.at[0], ep.at[0], 1, 1)
    put(eh.at[2], ep.at[2], 1, 0)
    put(mb.at[pl.ds(20, 8)], xm.at[0], 1, 0)
    put(sh.at[pl.ds(9, 18)], xc.at[0, pl.ds(9, 18)], 1, 0)

    for c in loads[6:]:
        c.wait()
    for x, steps in ((3, (2,)), (2, (1, 2)), (1, range(3)), (0, range(3))):
        pack_cotangent(x, steps, lambda q: row(cot, q, x))
    collide_row(1)
    collide_row(0)
    for r in range(4):
        store_sums(r)
    left, right = packed()
    for k in range(3):
        ey[k, 0] = left[k]
        ey[k, 1] = right[k]
    rest = (lane % 8 > 0) & (lane % 8 < 4)
    left = [jnp.where(rest, v, 0.0) for v in left]
    right = [jnp.where(rest, v, 0.0) for v in right]
    el[0] = right[0] + (rolly(right[1], 3) + rolly(right[2], 5))
    el[1] = left[0] + (rolly(left[1], 3) + rolly(left[2], 5))
    el[2] = left[0] + rolly(right[0], 3)

    for q in range(18):
        sl[q] = row(cot, q + 9, 0)
    for q in range(9):
        sl[q + 18] = row(cot, q + 18, 1)

    @pl.when(closes)
    def _():
        pl.semaphore_wait(straight, 1)

    put(ey.at[:, 1], en.at[0], 0, 1)
    put(ey.at[:, 0], en.at[1], 0, -1)
    slanting = [
        copy_to(el.at[0], ep.at[3], -1, 1),
        copy_to(el.at[1], ep.at[4], -1, -1),
    ]
    back = [
        copy_to(el.at[2], ep.at[5], -1, 0),
        copy_to(mb.at[pl.ds(2, 8)], xm.at[1], -1, 0),
        copy_to(sl, xc.at[1], -1, 0),
    ]

    @pl.when(jnp.logical_not(opens | closes))
    def _():
        pl.semaphore_wait(straight, 1)

    def send_back():
        for c in back:
            c.start()
        pl.semaphore_wait(aslant, 2)
        for c in slanting:
            c.start()

    @pl.when(jnp.logical_not(opens))
    def _():
        send_back()

    for n in range(27):
        rv[n] = jnp.full((8, 128), rates[n], F32)

    for c in soon:
        c.wait_recv()

    def known(n):
        return rv[n]

    def gn(x):
        return upper.at[x]

    packs = merged(en, ep, ey, False)
    exl, exr = packs[0][0], packs[1][0]
    for x in (4, 3, 2, 1):
        pull_row(x, exl, exr, known, cot, mb, xc, xm, gn(x))
    pull_beside(packs, known, gy)
    for x in (3, 2):
        pull_first(x, known, uck, mb, gn, gy, done.at[x - 1])

    @pl.when(opens)
    def _():
        pl.semaphore_wait(straight, 1)
        send_back()

    for c in late[:-1]:
        c.wait_recv()
    packs = merged(en, ep, ey, True)
    exl, exr = packs[0][0], packs[1][0]
    beside[0], beside[1] = exl, exr
    pull_row(0, exl, exr, known, cot, mb, xc, xm, gn(0))
    pull_beside(packs, known, gy)
    pull_first(1, known, uck, mb, gn, gy, done.at[0])
    late[-1].wait_recv()
    for c in copies:
        c.wait_send()


def finish(cot, mb, uck, rv, xc, xm, upper, gy, done, beside, out, lower, end, sems):
    def rates(n):
        return rv[n]

    def gn(x):
        return lower if x < 0 else upper.at[x]

    copies = []

    def put(src, x):
        copies.append(pltpu.make_async_copy(src, out.at[:, :, x], sems.at[x]))
        copies[-1].start()

    for x in (1, 2, 3):
        put(done.at[x - 1], x)
    pull_row(-1, beside[0], beside[1], rates, cot, mb, xc, xm, lower)
    pull_first(0, rates, uck, mb, gn, gy, end)
    put(end, 0)
    for c in copies:
        c.wait()


def shards(sizes, checkpoint, rates, wall_mask, cotangent):
    wall, rates = wall_mask.reshape(32, 128), rates.reshape(1, 27)
    vmem, hbm = pl.BlockSpec(memory_space=pltpu.VMEM), pl.BlockSpec(memory_space=pltpu.HBM)
    small = dict(vmem_limit_bytes=16 << 20)

    def like(*shape):
        return jax.ShapeDtypeStruct(shape, F32)

    got = pl.pallas_call(
        functools.partial(exchange, sizes),
        out_shape=(
            like(864, 128), like(30, 8, 128), like(4, 3, 8, 128), like(27, 8, 128), like(2, 27, 8, 128),
            like(2, 8, 8, 128), like(5, 27, 8, 128), like(27, 8, 128), like(3, 27, 8, 128), like(2, 8, 128),
        ),
        in_specs=[hbm] * 4,
        out_specs=(vmem,) * 10,
        scratch_shapes=[
            pltpu.VMEM((4, 27, 8, 128), F32),
            pltpu.VMEM((32, 128), jnp.int32),
            pltpu.SMEM((1, 27), F32),
            pltpu.VMEM((3, 2, 8, 128), F32),
            pltpu.VMEM((3, 8, 128), F32),
            pltpu.VMEM((3, 8, 128), F32),
            pltpu.VMEM((27, 8, 128), F32),
            pltpu.VMEM((27, 8, 128), F32),
            pltpu.VMEM((2, 3, 8, 128), F32),
            pltpu.VMEM((6, 8, 128), F32),
            pltpu.SemaphoreType.DMA((9,)),
            pltpu.SemaphoreType.REGULAR,
            pltpu.SemaphoreType.REGULAR,
            pltpu.SemaphoreType.DMA((13,)),
            pltpu.SemaphoreType.DMA((13,)),
        ],
        compiler_params=pltpu.CompilerParams(collective_id=0, has_side_effects=True, **small),
        name="exchange",
    )(*[pltpu.with_memory_space_constraint(v, pltpu.HBM) for v in (checkpoint, cotangent, wall, rates)])
    return pl.pallas_call(
        finish,
        out_shape=like(27, 8, 4, 128),
        in_specs=[vmem] * 10,
        out_specs=hbm,
        scratch_shapes=[
            pltpu.VMEM((27, 8, 128), F32),
            pltpu.VMEM((27, 8, 128), F32),
            pltpu.SemaphoreType.DMA((4,)),
        ],
        compiler_params=pltpu.CompilerParams(**small),
        name="finish",
    )(*got)


def solution(mesh):
    sizes = (mesh.shape["gx"], mesh.shape["gy"])
    in_specs = (P(None, None, "gx", "gy"), P(), P(None, "gx", "gy"), P(None, None, "gx", "gy"))
    out_specs = P(None, None, "gx", "gy")
    return jax.shard_map(
        functools.partial(shards, sizes), mesh=mesh, in_specs=in_specs, out_specs=out_specs, check_vma=False
    )
```

```python
import functools

import jax
import jax.numpy as jnp
from jax import lax
from jax.experimental import pallas as pl
from jax.experimental.pallas import tpu as pltpu
from jax.sharding import PartitionSpec as P

F32 = jnp.float32
MESH = pl.DeviceIdType.MESH
ROWS = 4
Q = [(a, b, c) for a in (-1, 0, 1) for b in (-1, 0, 1) for c in (-1, 0, 1)]
THIRD = 1.0 / 3.0
NINTH = 1.0 / 9.0


def rollz(v, s):
    return v if s == 0 else pltpu.roll(v, s % 8, 0)


def rolly(v, s):
    return v if s % 128 == 0 else pltpu.roll(v, s % 128, 1)


def lanes():
    return lax.broadcasted_iota(jnp.int32, (8, 128), 1)


def along(values, axis, fn):
    out = [None] * 27
    step = (9, 3, 1)[axis]
    for i in range(27):
        if (i // step) % 3 == 0:
            out[i], out[i + step], out[i + 2 * step] = fn(
                values[i], values[i + step], values[i + 2 * step]
            )
    return out


def to_moments(a, b, c):
    s = a + c
    return s + b, c - a, s


def from_halved(m0, m1, m2):
    a, c = m2 - m1, m2 + m1
    return a, m0 - (a + c), c


def dual_doubled(a, b, c):
    return b, c - a, (a + c) - (b + b)


def dual_back(m0, m1, m2):
    s = m0 + m2
    return s - m1, m0, s + m1


def at(i, j, k):
    return 9 * i + 3 * j + k


def halved_rates(rates_ref):
    return [
        rates_ref[0, n] * (0.5 ** sum(p > 0 for p in (n // 9, n // 3 % 3, n % 3)))
        for n in range(27)
    ]


def collide(f, rates, wall):
    m = f
    for axis in (2, 1, 0):
        m = along(m, axis, to_moments)
    rho, jx, jy, jz = m[0], m[9], m[3], m[1]
    inv = 1.0 / rho
    ux, uy, uz = jx * inv, jy * inv, jz * inv
    xx, yy, zz = jx * ux, jy * uy, jz * uz
    xy, xz, yz = jx * uy, jx * uz, jy * uz
    r3, r9 = rho * THIRD, rho * NINTH
    x3, y3, z3 = jx * THIRD, jy * THIRD, jz * THIRD
    eq = [None] * 27
    eq[at(0, 0, 0)] = rho
    eq[at(1, 0, 0)], eq[at(0, 1, 0)], eq[at(0, 0, 1)] = jx, jy, jz
    eq[at(2, 0, 0)], eq[at(0, 2, 0)], eq[at(0, 0, 2)] = r3 + xx, r3 + yy, r3 + zz
    eq[at(1, 1, 0)], eq[at(1, 0, 1)], eq[at(0, 1, 1)] = xy, xz, yz
    eq[at(1, 2, 0)] = eq[at(1, 0, 2)] = x3
    eq[at(2, 1, 0)] = eq[at(0, 1, 2)] = y3
    eq[at(2, 0, 1)] = eq[at(0, 2, 1)] = z3
    eq[at(1, 2, 2)], eq[at(2, 1, 2)], eq[at(2, 2, 1)] = x3 * THIRD, y3 * THIRD, z3 * THIRD
    eq[at(1, 1, 2)], eq[at(1, 2, 1)], eq[at(2, 1, 1)] = xy * THIRD, xz * THIRD, yz * THIRD
    eq[at(2, 2, 0)] = r9 + (xx + yy) * THIRD
    eq[at(2, 0, 2)] = r9 + (xx + zz) * THIRD
    eq[at(0, 2, 2)] = r9 + (yy + zz) * THIRD
    eq[at(2, 2, 2)] = r9 * THIRD + (xx + yy + zz) * NINTH
    d = [
        m[n] * rates[n] if eq[n] is None else (m[n] - eq[n]) * rates[n]
        for n in range(27)
    ]
    for axis in (0, 1, 2):
        d = along(d, axis, from_halved)
    solid = wall > 0.5
    out = [jnp.where(solid, f[26 - n], f[n] - d[n]) for n in range(27)]
    return out, (ux, uy, uz)


def pull_back(g, u, rates, wall, keep=range(27)):
    ux, uy, uz = u
    e = g
    for axis in (2, 1, 0):
        e = along(e, axis, dual_doubled)
    e = [e[n] * rates(n) for n in range(27)]
    e222 = e[at(2, 2, 2)] * NINTH
    pair_xy, pair_xz, pair_yz = e[at(2, 2, 0)], e[at(2, 0, 2)], e[at(0, 2, 2)]
    pxx = e[at(2, 0, 0)] + (pair_xy + pair_xz) * THIRD + e222
    pyy = e[at(0, 2, 0)] + (pair_xy + pair_yz) * THIRD + e222
    pzz = e[at(0, 0, 2)] + (pair_xz + pair_yz) * THIRD + e222
    pxy = e[at(1, 1, 0)] + e[at(1, 1, 2)] * THIRD
    pxz = e[at(1, 0, 1)] + e[at(1, 2, 1)] * THIRD
    pyz = e[at(0, 1, 1)] + e[at(2, 1, 1)] * THIRD
    rho = (
        e[0]
        + (e[at(2, 0, 0)] + e[at(0, 2, 0)] + e[at(0, 0, 2)] + e222) * THIRD
        + (pair_xy + pair_xz + pair_yz) * NINTH
    )
    cx = e[at(1, 0, 0)] + (e[at(1, 2, 0)] + e[at(1, 0, 2)]) * THIRD + e[at(1, 2, 2)] * NINTH
    cy = e[at(0, 1, 0)] + (e[at(2, 1, 0)] + e[at(0, 1, 2)]) * THIRD + e[at(2, 1, 2)] * NINTH
    cz = e[at(0, 0, 1)] + (e[at(2, 0, 1)] + e[at(0, 2, 1)]) * THIRD + e[at(2, 2, 1)] * NINTH
    sx = (pxx + pxx) * ux + pxy * uy + pxz * uz
    sy = (pyy + pyy) * uy + pxy * ux + pyz * uz
    sz = (pzz + pzz) * uz + pxz * ux + pyz * uy
    rho = rho - 0.5 * (ux * sx + uy * sy + uz * sz)
    e[at(0, 0, 0)] = e[at(0, 0, 0)] - rho
    e[at(1, 0, 0)] = e[at(1, 0, 0)] - (cx + sx)
    e[at(0, 1, 0)] = e[at(0, 1, 0)] - (cy + sy)
    e[at(0, 0, 1)] = e[at(0, 0, 1)] - (cz + sz)
    for axis in (2, 1, 0):
        e = along(e, axis, dual_back)
    solid = wall > 0.5
    return {n: jnp.where(solid, g[26 - n], g[n] - e[n]) for n in keep}


def row(ref, q, x):
    return ref[pl.ds(q * 32 + x, 8, stride=4), :]


def wall_row(ref, x):
    height = lax.broadcasted_iota(jnp.int32, (8, 128), 0)
    mask = ref[pl.ds(x, 8, stride=4), :]
    return jnp.where((height == 0) | (height == 7), 1, mask).astype(F32)


def upper_end(v, k):
    return jnp.where(lanes() % 8 >= (6 if k == 2 else 5), rolly(v, (4, 1, -1)[k]), 0.0)


def lower_end(v, k):
    return jnp.where(lanes() % 8 < (2 if k == 2 else 3), rolly(v, (-4, -1, -7)[k]), 0.0)


def merged(en, ep, ey):
    exl = [en[0, k] + upper_end(ep[3], k) for k in range(3)]
    exr = [en[1, k] + upper_end(ep[4], k) for k in range(3)]
    return exl, exr, ey[0, 0] + upper_end(ep[5], 0), ey[0, 1] + upper_end(ep[5], 1)


def completed(packs, ep):
    exl, exr, oxl, oxr = packs
    exl = [exl[k] + lower_end(ep[0], k) for k in range(3)]
    exr = [exr[k] + lower_end(ep[1], k) for k in range(3)]
    return exl, exr, oxl + lower_end(ep[2], 0), oxr + lower_end(ep[2], 1)


def field(r, k):
    if r == 0:
        return {0: 2, 2: 3, 3: 4, 1: 0, 4: 1}[k]
    return 5 * r + {0: 0, 2: 1, 3: 2, 1: 3, 4: 4}[k]


def slot(q):
    return 3 * (q // 9) + q % 3


def pull_beside(packs, rates, gy):
    exl, exr, oxl, oxr = packs
    lane = lanes()
    left = lane < 8
    g = []
    for q, (cx, cy, cz) in enumerate(Q):
        s = slot(q)
        lo, hi = ((exl[2], oxr), (exl[1], exr[1]), (oxl, exr[2]))[cy + 1]
        v = jnp.where(left, rolly(lo, -8 * s - cx), rolly(hi, 8 - 8 * s - cx))
        g.append(rollz(v, -cz))
    m = []
    lo, hi = exl[1] + oxl, exr[1] + oxr
    for k in range(4):
        s = 9 + k
        m.append(jnp.where(left, rolly(lo, -8 * s), rolly(hi, 8 - 8 * s)))
    w = jnp.where(left, rolly(exl[1], -104), rolly(exr[1], -96))
    cell = (lane < 16) & (lane % 8 > 0) & (lane % 8 < 7)
    inv = 1.0 / jnp.where(cell, m[0], 1.0)
    got = pull_back(g, [m[k] * inv for k in (1, 2, 3)], rates, w)
    for q, (cx, cy, cz) in enumerate(Q):
        if cy != 0:
            gy[q] = got[q]


def pull_row(x, exl, exr, rates, cot, mb, xc, xm, gn):
    lane = lanes()
    first, last = lane == 0, lane == 127

    def source(q, x):
        if 0 <= x < ROWS:
            return row(cot, q, x)
        if x == -1:
            return xc[0, q]
        if x == -2:
            return xc[0, 18 + q]
        return xc[1, q - 9] if x == ROWS else xc[1, q]

    m = []
    for k in range(4):
        v = mb[field(x + 1, k)]
        if x == -1:
            v = v + xm[0, field(1, k) - 5]
        if x == 0:
            v = v + xm[0, field(1, 0 if k == 1 else k)]
        if x == 3:
            v = v - xm[1, 0] if k == 1 else v + xm[1, field(0, k) - 2]
        if x == 4:
            v = v + xm[1, field(1, k) - 2]
        d = 8 * (9 + k) + x + 2
        v = v + jnp.where(first, rolly(exl, -d), 0.0)
        v = v + jnp.where(last, rolly(exr, 127 - d), 0.0)
        m.append(v)
    w = xm[0, 4] if x < 0 else xm[1, 7] if x == ROWS else mb[field(x + 1, 4)]
    g = []
    for q, (cx, cy, cz) in enumerate(Q):
        v = source(q, x + cx)
        d = 8 * slot(q) + x + cx + 2
        if cy == 1:
            v = jnp.where(last, rolly(exr, 127 - d), rolly(v, -1))
        if cy == -1:
            v = jnp.where(first, rolly(exl, -d), rolly(v, 1))
        g.append(rollz(v, -cz))
    inv = 1.0 / m[0]
    keep = range(9) if x < 0 else range(18, 27) if x == ROWS else range(27)
    got = pull_back(g, [m[k] * inv for k in (1, 2, 3)], rates, w, keep)
    for q in keep:
        gn[q] = got[q]


def pull_first(x, rates, uck, mb, gn, gy, out):
    lane = lanes()
    first, last = lane == 0, lane == 127
    g = []
    for q, (cx, cy, cz) in enumerate(Q):
        v = gn(x + cx)[q]
        d = x + cx + 2
        if cy == 1:
            v = jnp.where(last, rolly(gy[q], 127 - 8 - d), rolly(v, -1))
        if cy == -1:
            v = jnp.where(first, rolly(gy[q], -d), rolly(v, 1))
        g.append(rollz(v, -cz))
    got = pull_back(g, [uck[x, k] for k in range(3)], rates, mb[field(x + 1, 4)])
    for q in range(27):
        out[q] = got[q]


def exchange(
    sizes, ck_hbm, cot_hbm, wall_hbm, rates_hbm,
    cot, mb, uck, rv, xc, xm, upper, gy, done, beside,
    ck, wall, rates_ref, ey, eh, el, sh, sl, en, ep, load, straight, aslant, send, recv,
):
    nx, ny = sizes
    lane = lanes()

    def device(dx, dy):
        return (
            lax.rem(lax.axis_index("gx") + (dx + nx), nx),
            lax.rem(lax.axis_index("gy") + (dy + ny), ny),
        )

    def signal(sem, dx, steps):
        for dy in steps:
            pl.semaphore_signal(sem, inc=1, device_id=device(dx, dy), device_id_type=MESH)

    loads = []
    for src, dst in (
        (rates_hbm, rates_ref),
        (wall_hbm, wall),
        (ck_hbm.at[:, :, 3], ck.at[3]),
        (ck_hbm.at[:, :, 2], ck.at[2]),
        (cot_hbm.at[pl.ds(0, 18), :, 3], sh.at[pl.ds(0, 18)]),
        (cot_hbm.at[pl.ds(0, 9), :, 2], sh.at[pl.ds(18, 9)]),
        (cot_hbm.reshape(864, 128), cot),
        (ck_hbm.at[:, :, 1], ck.at[1]),
        (ck_hbm.at[:, :, 0], ck.at[0]),
    ):
        loads.append(pltpu.make_async_copy(src, dst, load.at[len(loads)]))
        loads[-1].start()

    place = lax.rem(lax.axis_index("gx"), nx // 2)
    opens, closes = place == 0, place == nx // 2 - 1
    barrier = pltpu.get_barrier_semaphore()
    signal(barrier, -1, (0, 1, -1))

    @pl.when(jnp.logical_not(closes))
    def _():
        signal(barrier, 0, (1, -1))

    @pl.when(closes)
    def _():
        pl.semaphore_wait(barrier, 3)

    @pl.when(jnp.logical_not(closes))
    def _():
        pl.semaphore_wait(barrier, 5)


    copies, late, soon = [], [], []

    def copy_to(src, dst, dx, dy):
        n = len(copies)
        copies.append(
            pltpu.make_async_remote_copy(
                src_ref=src,
                dst_ref=dst,
                send_sem=send.at[n],
                recv_sem=recv.at[n],
                device_id=device(dx, dy),
                device_id_type=MESH,
            )
        )
        (late if dx == 1 else soon).append(copies[-1])
        return copies[-1]

    def put(src, dst, dx, dy):
        copy_to(src, dst, dx, dy).start()

    put(cot_hbm.at[pl.ds(0, 9), :, 3], xc.at[0, pl.ds(0, 9)], 1, 0)
    signal(straight, 1, (0,))
    signal(aslant, 1, (1, -1))
    zero = jnp.zeros((8, 128), F32)
    first, last = lane == 0, lane == 127
    body = [[zero] * 4 for _ in range(6)]
    edge = [[zero] * 3 for _ in range(6)]
    acc = dict.fromkeys(("r0", "r1", "r2", "l0", "l1", "l2", "l0m"), zero)

    def add(name, v, d):
        acc[name] = jnp.where(lane == d, v, acc[name])

    def pack_cotangent(x, steps, get):
        for cx, cz in [(a, c) for a in steps for c in range(3)]:
            d = 8 * (3 * cx + cz) + x + 2
            v = rolly(get(at(cx, 0, cz)), d - 127)
            add("r0", v, d)
            add("r2", v, d - 1)
            v = rolly(get(at(cx, 2, cz)), d)
            add("l0", v, d)
            add("l2", v, d + 1)
            v = rolly(get(at(cx, 1, cz)), d - 127)
            add("r1", v, d)
            add("l1", v, d + 1)

    def pack_sums(r):
        outer = edge[r]
        outer = [outer[0], outer[1], jnp.where(first, outer[0], -outer[0]), outer[2]]
        for k in range(4):
            d = 8 * (9 + k) + r + 1
            v = rolly(body[r][k], d - 127)
            add("r1", v, d)
            add("l1", v, d + 1)
            v = rolly(outer[k], d)
            add("r0", v, d)
            add("l0m", v, d - 1)

    def pack_wall(x, w):
        d = 8 * 13 + x + 2
        v = rolly(w, d - 127)
        add("r1", v, d)
        add("l1", v, d + 1)

    def packed():
        left = acc["l0"] + rolly(acc["l0m"], 1), rolly(acc["l1"], -1), rolly(acc["l2"], -1)
        right = acc["r0"], acc["r1"], rolly(acc["r2"], 1)
        return left, right

    def collide_row(x):
        w = wall_row(wall, x)
        mb[field(x + 1, 4)] = w
        pack_wall(x, w)
        out, u = collide([ck[x, q] for q in range(27)], rates, w)
        for k in range(3):
            uck[x, k] = u[k]
        for a in range(3):
            sums, tilts = [], []
            for b in range(3):
                up = rollz(out[at(a, b, 2)], 1)
                down = rollz(out[at(a, b, 0)], -1)
                sums.append(out[at(a, b, 1)] + (up + down))
                tilts.append(up - down)
            ap, am = rolly(sums[2], 1), rolly(sums[0], -1)
            bp, bm = rolly(tilts[2], 1), rolly(tilts[0], -1)
            r = x + a
            outer = jnp.where(first, ap, am)
            edge[r][0] = edge[r][0] + outer
            edge[r][1] = edge[r][1] + (a - 1) * outer if a != 1 else edge[r][1]
            edge[r][2] = edge[r][2] + jnp.where(first, bp, bm)
            ap, am = jnp.where(first, 0.0, ap), jnp.where(last, 0.0, am)
            bp, bm = jnp.where(first, 0.0, bp), jnp.where(last, 0.0, bm)
            total = sums[1] + (ap + am)
            body[r][0] = body[r][0] + total
            if a != 1:
                body[r][1] = body[r][1] + (a - 1) * total
            body[r][2] = body[r][2] + (ap - am)
            body[r][3] = body[r][3] + (tilts[1] + (bp + bm))

    def store_sums(r):
        for k in range(4):
            mb[field(r, k)] = body[r][k]
        pack_sums(r)

    for c in loads[:6]:
        c.wait()
    pack_cotangent(3, (0, 1), lambda q: sh[q])
    pack_cotangent(2, (0,), lambda q: sh[q + 18])
    rates = halved_rates(rates_ref)
    collide_row(3)
    collide_row(2)
    store_sums(5)
    store_sums(4)
    left, right = packed()
    eh[0] = right[0] + (rolly(right[1], -3) + rolly(right[2], 3))
    eh[1] = left[0] + (rolly(left[1], -3) + rolly(left[2], 3))
    eh[2] = left[0] + rolly(right[0], -3)
    put(eh.at[1], ep.at[1], 1, -1)
    put(eh.at[0], ep.at[0], 1, 1)
    put(eh.at[2], ep.at[2], 1, 0)
    put(mb.at[pl.ds(20, 8)], xm.at[0], 1, 0)
    put(sh.at[pl.ds(9, 18)], xc.at[0, pl.ds(9, 18)], 1, 0)

    for c in loads[6:]:
        c.wait()
    for x, steps in ((3, (2,)), (2, (1, 2)), (1, range(3)), (0, range(3))):
        pack_cotangent(x, steps, lambda q: row(cot, q, x))
    collide_row(1)
    collide_row(0)
    for r in range(4):
        store_sums(r)
    left, right = packed()
    for k in range(3):
        ey[k, 0] = left[k]
        ey[k, 1] = right[k]
    rest = (lane % 8 > 0) & (lane % 8 < 4)
    left = [jnp.where(rest, v, 0.0) for v in left]
    right = [jnp.where(rest, v, 0.0) for v in right]
    el[0] = right[0] + (rolly(right[1], 3) + rolly(right[2], 5))
    el[1] = left[0] + (rolly(left[1], 3) + rolly(left[2], 5))
    el[2] = left[0] + rolly(right[0], 3)

    for q in range(18):
        sl[q] = row(cot, q + 9, 0)
    for q in range(9):
        sl[q + 18] = row(cot, q + 18, 1)

    @pl.when(closes)
    def _():
        pl.semaphore_wait(straight, 1)

    put(ey.at[:, 1], en.at[0], 0, 1)
    put(ey.at[:, 0], en.at[1], 0, -1)
    slanting = [
        copy_to(el.at[0], ep.at[3], -1, 1),
        copy_to(el.at[1], ep.at[4], -1, -1),
    ]
    back = [
        copy_to(el.at[2], ep.at[5], -1, 0),
        copy_to(mb.at[pl.ds(2, 8)], xm.at[1], -1, 0),
        copy_to(sl, xc.at[1], -1, 0),
    ]

    @pl.when(jnp.logical_not(opens | closes))
    def _():
        pl.semaphore_wait(straight, 1)

    def send_back():
        for c in back:
            c.start()
        pl.semaphore_wait(aslant, 2)
        for c in slanting:
            c.start()

    @pl.when(jnp.logical_not(opens))
    def _():
        send_back()

    for n in range(27):
        rv[n] = jnp.full((8, 128), rates[n], F32)

    for c in soon:
        c.wait_recv()

    def known(n):
        return rv[n]

    def gn(x):
        return upper.at[x]

    packs = merged(en, ep, ey)
    exl, exr = packs[0][0], packs[1][0]
    for x in (4, 3, 2, 1):
        pull_row(x, exl, exr, known, cot, mb, xc, xm, gn(x))
    pull_beside(packs, known, gy)
    for x in (3, 2):
        pull_first(x, known, uck, mb, gn, gy, done.at[x - 1])

    @pl.when(opens)
    def _():
        pl.semaphore_wait(straight, 1)
        send_back()

    for c in copies:
        c.wait_send()
    for c in late[:-1]:
        c.wait_recv()
    packs = completed(packs, ep)
    exl, exr = packs[0][0], packs[1][0]
    beside[0], beside[1] = exl, exr
    pull_row(0, exl, exr, known, cot, mb, xc, xm, gn(0))
    pull_beside(packs, known, gy)
    pull_first(1, known, uck, mb, gn, gy, done.at[0])
    late[-1].wait_recv()


def finish(cot, mb, uck, rv, xc, xm, upper, gy, done, beside, out, lower, end, sems):
    def rates(n):
        return rv[n]

    def gn(x):
        return lower if x < 0 else upper.at[x]

    copies = []

    def put(src, x):
        copies.append(pltpu.make_async_copy(src, out.at[:, :, x], sems.at[x]))
        copies[-1].start()

    for x in (1, 2, 3):
        put(done.at[x - 1], x)
    pull_row(-1, beside[0], beside[1], rates, cot, mb, xc, xm, lower)
    pull_first(0, rates, uck, mb, gn, gy, end)
    put(end, 0)
    for c in copies:
        c.wait()


def shards(sizes, checkpoint, rates, wall_mask, cotangent):
    wall, rates = wall_mask.reshape(32, 128), rates.reshape(1, 27)
    vmem, hbm = pl.BlockSpec(memory_space=pltpu.VMEM), pl.BlockSpec(memory_space=pltpu.HBM)
    small = dict(vmem_limit_bytes=16 << 20)

    def like(*shape):
        return jax.ShapeDtypeStruct(shape, F32)

    got = pl.pallas_call(
        functools.partial(exchange, sizes),
        out_shape=(
            like(864, 128), like(30, 8, 128), like(4, 3, 8, 128), like(27, 8, 128), like(2, 27, 8, 128),
            like(2, 8, 8, 128), like(5, 27, 8, 128), like(27, 8, 128), like(3, 27, 8, 128), like(2, 8, 128),
        ),
        in_specs=[hbm] * 4,
        out_specs=(vmem,) * 10,
        scratch_shapes=[
            pltpu.VMEM((4, 27, 8, 128), F32),
            pltpu.VMEM((32, 128), jnp.int32),
            pltpu.SMEM((1, 27), F32),
            pltpu.VMEM((3, 2, 8, 128), F32),
            pltpu.VMEM((3, 8, 128), F32),
            pltpu.VMEM((3, 8, 128), F32),
            pltpu.VMEM((27, 8, 128), F32),
            pltpu.VMEM((27, 8, 128), F32),
            pltpu.VMEM((2, 3, 8, 128), F32),
            pltpu.VMEM((6, 8, 128), F32),
            pltpu.SemaphoreType.DMA((9,)),
            pltpu.SemaphoreType.REGULAR,
            pltpu.SemaphoreType.REGULAR,
            pltpu.SemaphoreType.DMA((13,)),
            pltpu.SemaphoreType.DMA((13,)),
        ],
        compiler_params=pltpu.CompilerParams(collective_id=0, has_side_effects=True, **small),
        name="exchange",
    )(*[pltpu.with_memory_space_constraint(v, pltpu.HBM) for v in (checkpoint, cotangent, wall, rates)])
    return pl.pallas_call(
        finish,
        out_shape=like(27, 8, 4, 128),
        in_specs=[vmem] * 10,
        out_specs=hbm,
        scratch_shapes=[
            pltpu.VMEM((27, 8, 128), F32),
            pltpu.VMEM((27, 8, 128), F32),
            pltpu.SemaphoreType.DMA((4,)),
        ],
        compiler_params=pltpu.CompilerParams(**small),
        name="finish",
    )(*got)


def solution(mesh):
    sizes = (mesh.shape["gx"], mesh.shape["gy"])
    in_specs = (P(None, None, "gx", "gy"), P(), P(None, "gx", "gy"), P(None, None, "gx", "gy"))
    out_specs = P(None, None, "gx", "gy")
    return jax.shard_map(
        functools.partial(shards, sizes), mesh=mesh, in_specs=in_specs, out_specs=out_specs, check_vma=False
    )
```
